256 devices in a mesh: row: 8 (over y, core), col: 32 (over z, x).
Axes of the slice: x: 4, y: 4, z: 8, core: 2. Of those that a mesh axis runs over, the one named last changes fastest.
Arguments:
- ancestor: bfloat16 [16384, 16384], P('row', 'col'), may hold values from -6 to 6, as said below
- panels: bfloat16 [3, 512, 16384], P(None, 'col', 'row'), may hold values from -0.0625 to 0.0625
- diag_inverse: float32 [3, 512, 512], replicated, may hold values from -6 to 6, as said below
- supernode_blocks: int32 [3, 4], replicated, may hold values from 0 to 127, as said below
- row_lists: int32 [3, 64], replicated, may hold values from 0 to 127, as said below
Outputs:
- updated: bfloat16 [16384, 16384], P('row', 'col')
The draws below stay inside these ranges and needn't reach their ends.
Inputs may be any that keep to these rules, and one draw needn't show every extreme that they name: ancestor is exactly symmetric. `diag_inverse`: each supernode's block is exactly symmetric. `supernode_blocks`: the 3 times 512 / 128 block numbers are all distinct. `row_lists`: each row holds 64 distinct block numbers; row s holds every block of the supernodes before s and none of supernode s or of later ones.
All inputs are finite; a program needn't handle non-finite values.
Results may differ from the reference program's by a relative error of at most 0.002.
Values may be sent and summed in bfloat16 or wider, within the bound.
No kernel may reach another device: no remote copies, remote signals or barrier semaphores. Data moves between devices by JAX's collectives and lax.ppermute only.
A program may use at most 64 MiB of HBM per device.

```python
import jax
import jax.numpy as jnp
from jax import lax

M = 16384
W = 512
B = 128
S = 3
LEN = 64


def block_layout(key):
    base_key = jax.random.fold_in(key, 11)
    perm_key, score_key = jax.random.split(base_key)
    blocks = M // B
    per_node = W // B
    block_ids = jnp.arange(blocks, dtype=jnp.int32)
    inner_ids = jnp.arange(blocks - 2, dtype=jnp.int32) + 1
    shuffle = jax.random.permutation(perm_key, inner_ids)
    first_end = jnp.zeros((1,), jnp.int32)
    last_end = jnp.full((1,), blocks - 1, jnp.int32)
    picked_all = jnp.concatenate([first_end, shuffle[:S * per_node - 2].astype(jnp.int32), last_end])
    chosen = picked_all.reshape(S, per_node).astype(jnp.int32)
    picked_lists = []
    for supernode in range(S):
        noise_draw = jax.random.randint(jax.random.fold_in(score_key, supernode), (blocks,), 0, 2 * blocks, dtype=jnp.int32)
        scores = (noise_draw - block_ids + blocks) * blocks + block_ids
        earlier = jnp.any(block_ids[:, None] == chosen[:supernode].reshape(-1)[None, :], axis=1)
        later = jnp.any(block_ids[:, None] == chosen[supernode:].reshape(-1)[None, :], axis=1)
        scores = jnp.where(earlier, 2 ** 28 + block_ids, scores)
        scores = jnp.where(later, block_ids - 2 ** 28, scores)
        picked = lax.top_k(scores, LEN)[1].astype(jnp.int32)
        picked_lists.append(picked)
    return (chosen, jnp.stack(picked_lists).astype(jnp.int32))


def draw_supernode_blocks(key, part):
    return block_layout(key)[0]


def draw_row_lists(key, part):
    return block_layout(key)[1]


def draw_ancestor(key, part):
    sample = jnp.clip(jax.random.normal(key, (M, M), jnp.float32), -4.0, 4.0)
    return ((sample + sample.T) * 0.70710678).astype(jnp.bfloat16)


def draw_diag_inverse(key, part):
    sample = jnp.clip(jax.random.normal(key, (S, W, W), jnp.float32), -4.0, 4.0)
    return ((sample + jnp.swapaxes(sample, 1, 2)) * 0.70710678).astype(jnp.float32)


def level_of(key, extent, pieces, low, top_value):
    loudness, own = 1.0, jax.random.fold_in(key, 6)
    for axis_at, parts in pieces:
        draws = jnp.exp(jax.random.uniform(jax.random.fold_in(own, axis_at), (parts,), jnp.float32, low / len(pieces), top_value / len(pieces)))
        loudness = loudness * jnp.repeat(draws, extent[axis_at] // parts).reshape([-1 if axis == axis_at else 1 for axis in range(len(extent))])
    return loudness


def scatter_about(own_key, extent, scale, limit, cuts=(), kind=jnp.bfloat16):
    values = scale * jax.random.normal(own_key, extent, jnp.float32)
    if cuts:
        values = values * level_of(own_key, extent, cuts, -0.22, 0.18)
    return jnp.clip(values, -limit, limit).astype(kind)


def setup_inputs(seed: int = 0) -> dict:
    seeds = jax.random.split(jax.random.key(seed), 6)
    ancestor = draw_ancestor(jax.random.fold_in(seeds[5], 71), 0)
    panels = scatter_about(seeds[1], (S, W, M), (LEN * B) ** -0.5, 0.0625, ((1, 32), (2, 8)))
    diag_inverse = draw_diag_inverse(jax.random.fold_in(seeds[5], 71), 0)
    supernode_blocks = draw_supernode_blocks(jax.random.fold_in(seeds[5], 71), 0)
    row_lists = draw_row_lists(jax.random.fold_in(seeds[5], 71), 0)
    return {"ancestor": ancestor, "panels": panels, "diag_inverse": diag_inverse, "supernode_blocks": supernode_blocks, "row_lists": row_lists}


def reference(ancestor, panels, diag_inverse, supernode_blocks, row_lists):
    offsets = jnp.arange(B, dtype=jnp.int32)
    current = ancestor
    for supernode in range(S):
        row_index = (row_lists[supernode][:, None] * B + offsets[None, :]).reshape(-1).astype(jnp.int32)
        col_index = (supernode_blocks[supernode][:, None] * B + offsets[None, :]).reshape(-1).astype(jnp.int32)
        selected = current[row_index][:, row_index].astype(jnp.float32)
        panel_rows = panels[supernode][:, row_index].astype(jnp.float32)
        update = (-jnp.dot(selected, panel_rows.T, preferred_element_type=jnp.float32)).astype(jnp.bfloat16)
        cross_term = jnp.dot(panel_rows, update.astype(jnp.float32), preferred_element_type=jnp.float32)
        diag_block = (diag_inverse[supernode] - 0.5 * (cross_term + cross_term.T)).astype(jnp.bfloat16)
        column = jnp.zeros((M, W), jnp.bfloat16).at[row_index].set(update).at[col_index].set(diag_block)
        current = current.at[:, col_index].set(column)
        current = current.at[col_index, :].set(column.T)
    return current
```

```python
import jax
import jax.numpy as jnp
from jax import lax
from jax.experimental import pallas as pl
from jax.experimental.pallas import tpu as pltpu
from jax.sharding import Mesh, PartitionSpec as P

S = 3
NODE = 4
NY, NC, NZ, NX = 4, 2, 8, 4
SIZES = {"y": NY, "core": NC, "z": NZ, "x": NX}
BF = jnp.bfloat16
F32 = jnp.float32
PAIRS = ((0, 0), (1, 0), (1, 1), (2, 0), (2, 1), (2, 2))
INTERPRET = False


def send(value, axis, step):
    size = SIZES[axis]
    return lax.ppermute(value, axis, [(i, (i + step) % size) for i in range(size)])


def ring_gather(value, axis):
    size = SIZES[axis]
    found = [None] * size
    found[0] = value
    ahead = behind = value
    for step in range(1, size // 2):
        behind = send(behind, axis, 1)
        ahead = send(ahead, axis, -1)
        found[step] = ahead
        found[size - step] = behind
    half = value.shape[0] // 2
    found[size // 2] = jnp.concatenate(
        [send(behind[:half], axis, 1), send(ahead[half:], axis, -1)], axis=0
    )
    return found


def to_absolute(relative, axis, position):
    size = relative.shape[axis]
    twice = jnp.concatenate([relative, relative], axis=axis)
    return lax.dynamic_slice_in_dim(twice, size - position, size, axis=axis)


def direct_scatter_sum(value, axis, position, extent, dim, kind=BF):
    size = SIZES[axis]

    def piece(owner):
        return lax.dynamic_slice_in_dim(value, owner * extent, extent, axis=dim)

    total = piece(position)
    for step in range(1, size):
        total = total + send(piece((position + step) % size).astype(kind), axis, step).astype(F32)
    return total


def by_core(core, first, second):
    return jnp.where(core == 0, first, second)


def finish_kernel(rs, cs, pos, a_ref, ut_ref, g0, g1, g2, g3, k0, k1, k2, k3, out_ref):
    block = a_ref.shape[0]
    row = rs[pl.program_id(0)]
    for j, (g, kk) in enumerate(zip((g0, g1, g2, g3), (k0, k1, k2, k3))):
        col = cs[j]
        span = slice(j * block, (j + 1) * block)

        @pl.when((row < 0) & (col < 0))
        def _():
            out_ref[:, span] = a_ref[:, span]

        @pl.when((row < 0) & (col >= 0))
        def _():
            out_ref[:, span] = g[...].reshape(block, block).astype(F32).T.astype(BF)

        @pl.when((row >= 0) & (col < 0))
        def _():
            out_ref[:, span] = ut_ref[:, span]

        @pl.when((row >= 0) & (col >= 0))
        def _():
            out_ref[:, span] = kk[...]


def finish(ancestor, ut, gathered, corner, row_index, col_index, z, x):
    rows, cols = ancestor.shape
    block = cols // NODE

    def g_map(j):
        def index(i, rs, cs, pos):
            col = jnp.maximum(cs[j], 0)
            z_from = 2 * (i % 4) + (col % 4) // 2
            dz = (z_from - pos[0] + NZ) % NZ
            dx = (i // 4 - pos[1] + NX) % NX
            on = cs[j] >= 0
            zero = jnp.int32(0)
            return (
                jnp.where(on, col // 4, zero),
                jnp.where(on, dz, zero),
                jnp.where(on, dx, zero),
                jnp.where(on, col % 2, zero),
                zero,
            )

        return index

    def k_map(j):
        def index(i, rs, cs, pos):
            return (jnp.maximum(rs[i], 0), jnp.maximum(cs[j], 0))

        return index

    spec = pltpu.PrefetchScalarGridSpec(
        num_scalar_prefetch=3,
        grid=(rows // block,),
        in_specs=[
            pl.BlockSpec((block, cols), lambda i, rs, cs, pos: (i, 0)),
            pl.BlockSpec((block, cols), lambda i, rs, cs, pos: (jnp.maximum(rs[i], 0), 0)),
            *[pl.BlockSpec((1, 1, 1, block, block), g_map(j)) for j in range(NODE)],
            *[pl.BlockSpec((block, block), k_map(j)) for j in range(NODE)],
        ],
        out_specs=pl.BlockSpec((block, cols), lambda i, rs, cs, pos: (i, 0)),
    )
    return pl.pallas_call(
        finish_kernel,
        out_shape=jax.ShapeDtypeStruct((rows, cols), BF),
        grid_spec=spec,
        interpret=INTERPRET,
    )(
        row_index,
        col_index,
        jnp.stack([z, x]).astype(jnp.int32),
        ancestor,
        ut,
        *[gathered] * NODE,
        *[corner] * NODE,
    )


def contract(left, right, dims):
    return lax.dot_general(left, right, (dims, ((), ())), preferred_element_type=F32)


def mm(left, right):
    return contract(left, right, ((1,), (0,)))


def mmt(left, right):
    return contract(left, right, ((1,), (1,)))


def corner_chain(cross, diag_inverse, w10, w20, w21):
    def diagonal(s, value):
        return (diag_inverse[s] - 0.5 * (value + value.T)).astype(BF)

    c = {pair: cross[i].astype(F32) for i, pair in enumerate(PAIRS)}
    d0 = diagonal(0, c[0, 0])
    u10 = (-(c[1, 0] + mm(w10, d0))).astype(BF)
    d1 = diagonal(1, c[1, 1] + mmt(w10, u10))
    u20 = (-(c[2, 0] + mm(w20, d0) + mm(w21, u10))).astype(BF)
    u21 = (-(c[2, 1] + mmt(w20, u10) + mm(w21, d1))).astype(BF)
    d2 = diagonal(2, c[2, 2] + mmt(w20, u20) + mmt(w21, u21))
    return jnp.concatenate(
        [
            jnp.concatenate([d0, u10.T, u20.T], axis=1),
            jnp.concatenate([u10, d1, u21.T], axis=1),
            jnp.concatenate([u20, u21, d2], axis=1),
        ],
        axis=0,
    )


def local(ancestor, panels, diag_inverse, supernode_blocks, row_lists):
    y, core, z, x = (lax.axis_index(name) for name in ("y", "core", "z", "x"))
    rows, cols = ancestor.shape
    block = cols // NODE
    width = NODE * block
    half = width // 2
    wl = panels.shape[1]
    row_blocks = rows // block
    first_row = (2 * y + core) * row_blocks
    first_col = (NX * z + x) * NODE
    k_list = supernode_blocks.reshape(-1)

    row_ids = first_row + jnp.arange(row_blocks, dtype=jnp.int32)
    col_ids = first_col + jnp.arange(NODE, dtype=jnp.int32)
    numbers = jnp.arange(S * NODE, dtype=jnp.int32) + 1
    row_index = jnp.sum(jnp.where(row_ids[:, None] == k_list[None, :], numbers, 0), axis=1) - 1
    col_index = jnp.sum(jnp.where(col_ids[:, None] == k_list[None, :], numbers, 0), axis=1) - 1
    listed = jnp.any(row_ids[None, :, None] == row_lists[:, None, :], axis=2)

    with jax.named_scope("own_columns"):
        source = panels.reshape(S, wl, row_blocks, block)

        def owned(s, t):
            parts = []
            for k in range(NODE):
                at = supernode_blocks[t, k] - first_row
                parts.append(
                    sum(
                        jnp.where(at == b, source[s, :, b, :], jnp.zeros((), BF))
                        for b in range(row_blocks)
                    )
                )
            return jnp.concatenate(parts, axis=1)

        own = jnp.concatenate([owned(1, 0), owned(2, 0), owned(2, 1)], axis=1)
        lane_half = 3 * half
        own_kept = by_core(core, own[:, :lane_half], own[:, lane_half:])
        own_sent = by_core(core, own[:, lane_half:], own[:, :lane_half])
        own_kept = own_kept + send(own_sent, "core", 1)
        own_sum = own_kept
        for step in range(1, NY):
            own_sum = own_sum + send(own_kept, "y", step)

    with jax.named_scope("gather_panels"):
        masked = jnp.where(listed[:, None, :, None], source, jnp.zeros((), BF)).reshape(
            S, wl, rows
        )
        second = masked[1:].reshape(2 * wl, rows)
        second_z = ring_gather(second, "z")
        first = jnp.concatenate([masked[0], own_sum], axis=1)
        first_x = ring_gather(first, "x")
        first_zx = ring_gather(jnp.concatenate(first_x, axis=0), "z")
        second_zx = ring_gather(jnp.concatenate(second_z, axis=0), "x")

    with jax.named_scope("products"):
        active = jnp.where(
            (row_index < 0)[:, None, None], ancestor.reshape(row_blocks, block, cols), 0
        ).reshape(rows, cols)
        q_first = [mm(part[:, :rows], active) for part in first_zx]
        q_second = [mm(part, active) for part in second_zx]

    with jax.named_scope("reduce_products"):
        low = jnp.concatenate(q_first[: NZ // 2] + q_second[: NX // 2], axis=0)
        high = jnp.concatenate(q_first[NZ // 2 :] + q_second[NX // 2 :], axis=0)
        q_chip = by_core(core, low, high) + send(by_core(core, high, low), "core", 1)
        q_mine = direct_scatter_sum(q_chip, "y", y, block, 1)
        q_other = send(q_mine, "core", 1)
        q_low = by_core(core, q_mine, q_other)
        q_high = by_core(core, q_other, q_mine)
        cut = NZ // 2 * NX * wl
        q0 = jnp.concatenate([q_low[:cut], q_high[:cut]], axis=0).reshape(NZ, NX, wl, block)
        q12 = jnp.concatenate([q_low[cut:], q_high[cut:]], axis=0).reshape(
            NX, NZ, 2, wl, block
        )
        q0 = to_absolute(to_absolute(q0, 0, z), 1, x).reshape(width, block)
        q12 = to_absolute(to_absolute(q12, 1, z), 0, x).transpose(2, 1, 0, 3, 4)
        q12 = q12.reshape(2, width, block)
        own_mine = jnp.concatenate([part[:, rows:] for part in first_zx], axis=0)
        own_other = send(own_mine, "core", 1)
        own_all = jnp.concatenate(
            [by_core(core, own_mine, own_other), by_core(core, own_other, own_mine)], axis=1
        ).reshape(NZ, NX, wl, 3 * width)
        own_all = to_absolute(to_absolute(own_all, 0, z), 1, x).reshape(width, 3 * width)
        w10, w20, w21 = (own_all[:, i * width : (i + 1) * width] for i in range(3))

    with jax.named_scope("update"):
        my_block = first_col + y
        outside = jnp.all(my_block != k_list)
        keep = [jnp.any(my_block == row_lists[s]) & outside for s in range(S)]
        u0 = jnp.where(keep[0], -q0, 0.0).astype(BF)
        u1 = jnp.where(keep[1], -(q12[0] + mm(w10, u0)), 0.0).astype(BF)
        u2 = jnp.where(keep[2], -(q12[1] + mm(w20, u0) + mm(w21, u1)), 0.0).astype(BF)
        u = jnp.stack([u0, u1, u2])
        u_half = by_core(core, u[:, :half], u[:, half:])

    with jax.named_scope("turn"):
        pairs = []
        for fy in range(NY):
            for fc in range(NC):
                for fz in range(NZ):
                    target = ((fz // 2) * NC + fz % 2) * NZ + 2 * fy + fc
                    pairs.append(((fy * NC + fc) * NZ + fz, target))
        turned = lax.ppermute(u_half, ("y", "core", "z"), pairs)

    with jax.named_scope("inner"):
        lane = (NX * x + z // 2) * block

        def lanes(part):
            return lax.dynamic_slice_in_dim(part, lane, block, axis=1)

        p0 = jnp.concatenate([lanes(part) for part in first_zx], axis=0)
        p12 = jnp.concatenate([lanes(part) for part in second_zx], axis=0)
        p0 = to_absolute(to_absolute(p0.reshape(NZ, NX, wl, block), 0, z), 1, x)
        p12 = to_absolute(to_absolute(p12.reshape(NX, NZ, 2, wl, block), 1, z), 0, x)
        p12 = p12.transpose(2, 1, 0, 3, 4).reshape(2, width, block)
        p_rows = (p0.reshape(width, block), p12[0], p12[1])
        inner = [mmt(p_rows[s], turned[t]) for s, t in PAIRS]
        inner_a = jnp.concatenate(inner[:3], axis=0)
        inner_b = jnp.concatenate(inner[3:], axis=0)
        part = by_core(core, inner_a, inner_b) + send(by_core(core, inner_b, inner_a), "core", 1)
        part = direct_scatter_sum(part, "y", y, 3 * width // NY, 0)
        part = direct_scatter_sum(part, "x", x, 3 * width // (NY * NX), 0, F32)
        sent = part
        for step in (2, 4, 6):
            part = part + send(sent, "z", step)
        part = part.astype(BF)
        other = lax.ppermute(part, "z", [(i, i ^ 1) for i in range(NZ)])
        even = z % 2 == 0
        part = jnp.concatenate(
            [jnp.where(even, part, other), jnp.where(even, other, part)], axis=1
        )
        part = to_absolute(jnp.stack(ring_gather(part, "x")), 0, x).reshape(-1, width)
        part = to_absolute(jnp.stack(ring_gather(part, "y")), 0, y).reshape(-1, width)
        other = send(part, "core", 1)
        cross = jnp.concatenate([by_core(core, part, other), by_core(core, other, part)], axis=0)
        cross = cross.reshape(6, width, width)

    with jax.named_scope("columns"):
        flat0 = turned[0]
        flat12 = turned[1:].reshape(width, block)
        g_first = ring_gather(jnp.concatenate(ring_gather(flat0, "x"), axis=0), "z")
        g_second = ring_gather(jnp.concatenate(ring_gather(flat12, "z"), axis=0), "x")
        g_first = jnp.stack(g_first).reshape(1, NZ, NX, half, block)
        g_second = jnp.stack(g_second).reshape(NX, NZ, 2, half, block).transpose(2, 1, 0, 3, 4)
        gathered = jnp.concatenate([g_first, g_second], axis=0)

    with jax.named_scope("rows"):
        flat = u_half.reshape(3 * half, block)
        strip = to_absolute(jnp.stack(ring_gather(flat, "y")), 0, y)
        strip = strip.transpose(1, 0, 2).reshape(S, half, cols)
        other = send(strip, "core", 1)
        ut = jnp.concatenate(
            [by_core(core, strip, other), by_core(core, other, strip)], axis=1
        ).reshape(S * width, cols)

    with jax.named_scope("corner"):
        corner = corner_chain(cross, diag_inverse, w10, w20, w21)
    return finish(ancestor, ut, gathered, corner, row_index, col_index, z, x)


def solution(mesh):
    fine = Mesh(mesh.devices.reshape(NY, NC, NZ, NX), ("y", "core", "z", "x"))
    row, col = ("y", "core"), ("z", "x")
    in_specs = (P(row, col), P(None, col, row), P(), P(), P())
    return jax.shard_map(
        local, mesh=fine, in_specs=in_specs, out_specs=P(row, col), check_vma=False
    )
```

```python
import jax
import jax.numpy as jnp
from jax import lax
from jax.experimental import pallas as pl
from jax.experimental.pallas import tpu as pltpu
from jax.sharding import Mesh, PartitionSpec as P

S = 3
NODE = 4
NY, NC, NZ, NX = 4, 2, 8, 4
SIZES = {"y": NY, "core": NC, "z": NZ, "x": NX}
BF = jnp.bfloat16
F32 = jnp.float32
PAIRS = ((0, 0), (1, 0), (1, 1), (2, 0), (2, 1), (2, 2))
INTERPRET = False


def send(value, axis, step):
    size = SIZES[axis]
    return lax.ppermute(value, axis, [(i, (i + step) % size) for i in range(size)])


def ring_gather(value, axis):
    size = SIZES[axis]
    found = [None] * size
    found[0] = value
    ahead = behind = value
    for step in range(1, size // 2):
        behind = send(behind, axis, 1)
        ahead = send(ahead, axis, -1)
        found[step] = ahead
        found[size - step] = behind
    half = value.shape[0] // 2
    found[size // 2] = jnp.concatenate(
        [send(behind[:half], axis, 1), send(ahead[half:], axis, -1)], axis=0
    )
    return found


def place(found, axis, position, dim=0):
    size = SIZES[axis]
    out = None
    for step, part in enumerate(found):
        part = jnp.expand_dims(part, dim)
        if out is None:
            shape = list(part.shape)
            shape[dim] = size
            out = jnp.zeros(shape, part.dtype)
        out = lax.dynamic_update_slice_in_dim(out, part, (position + step) % size, axis=dim)
    return out


def direct_gather(value, axis):
    size = SIZES[axis]
    return [value] + [send(value, axis, size - step) for step in range(1, size)]


def direct_scatter_sum(value, axis, position, extent, dim, kind=BF):
    size = SIZES[axis]

    def piece(owner):
        return lax.dynamic_slice_in_dim(value, owner * extent, extent, axis=dim)

    total = piece(position)
    for step in range(1, size):
        total = total + send(piece((position + step) % size).astype(kind), axis, step).astype(F32)
    return total


def by_core(core, first, second):
    return jnp.where(core == 0, first, second)


def prepare_kernel(flags, at, p_ref, first_ref, second_ref, own_ref):
    wl = p_ref.shape[1]
    block = own_ref.shape[1] // (3 * NODE)
    row_blocks = p_ref.shape[2] // block
    for s in range(S):
        for b in range(row_blocks):
            span = slice(b * block, (b + 1) * block)
            value = p_ref[s, :, span]
            value = jnp.where(flags[s * row_blocks + b] > 0, value, jnp.zeros_like(value))
            if s == 0:
                first_ref[:, span] = value
            else:
                second_ref[(s - 1) * wl : s * wl, span] = value
    for pair, (s, t) in enumerate(((1, 0), (2, 0), (2, 1))):
        for k in range(NODE):
            index = at[t * NODE + k]
            inside = (index >= 0) & (index < row_blocks)
            start = pl.multiple_of(jnp.where(inside, index, 0) * block, block)
            value = p_ref[s, :, pl.ds(start, block)]
            value = jnp.where(inside, value, jnp.zeros_like(value))
            own_ref[:, (pair * NODE + k) * block : (pair * NODE + k + 1) * block] = value


def prepare(panels, listed, at, block):
    _, wl, rows = panels.shape
    return pl.pallas_call(
        prepare_kernel,
        out_shape=(
            jax.ShapeDtypeStruct((wl, rows), BF),
            jax.ShapeDtypeStruct((2 * wl, rows), BF),
            jax.ShapeDtypeStruct((wl, 3 * NODE * block), BF),
        ),
        in_specs=[
            pl.BlockSpec(memory_space=pltpu.SMEM),
            pl.BlockSpec(memory_space=pltpu.SMEM),
            pl.BlockSpec(memory_space=pltpu.VMEM),
        ],
        interpret=INTERPRET,
    )(listed.astype(jnp.int32).reshape(-1), at, panels)


def pick_kernel(index, ut_ref, out_ref):
    out_ref[0] = ut_ref[...]


def pick(index, ut, block):
    count = index.shape[0]
    cols = ut.shape[1]
    return pl.pallas_call(
        pick_kernel,
        out_shape=jax.ShapeDtypeStruct((count, block, cols), BF),
        grid_spec=pltpu.PrefetchScalarGridSpec(
            num_scalar_prefetch=1,
            grid=(count,),
            in_specs=[pl.BlockSpec((block, cols), lambda i, index: (index[i], 0))],
            out_specs=pl.BlockSpec((1, block, cols), lambda i, index: (i, 0, 0)),
        ),
        interpret=INTERPRET,
    )(index, ut)


def finish_kernel(rs, cs, pos, a_ref, ut_ref, g_ref, out_ref):
    cols = out_ref.shape[1]
    block = cols // NODE
    i = pl.program_id(0)
    for q in range(NODE):
        row = rs[i * NODE + q]
        here = slice(q * block, (q + 1) * block)
        source = pl.multiple_of(jnp.maximum(row, 0) * block, block)
        for j in range(NODE):
            col = cs[j]
            span = slice(j * block, (j + 1) * block)

            @pl.when((row < 0) & (col < 0))
            def _():
                out_ref[here, span] = a_ref[here, span]

            @pl.when((row < 0) & (col >= 0))
            def _():
                out_ref[here, span] = g_ref[0, j, :, here].astype(F32).T.astype(BF)

            @pl.when(row >= 0)
            def _():
                out_ref[here, span] = ut_ref[pl.ds(source, block), span]


def finish(ancestor, ut, columns, row_index, col_index, x):
    rows, cols = ancestor.shape
    block = cols // NODE
    spec = pltpu.PrefetchScalarGridSpec(
        num_scalar_prefetch=3,
        grid=(NX,),
        in_specs=[
            pl.BlockSpec((rows // NX, cols), lambda i, rs, cs, pos: (i, 0)),
            pl.BlockSpec(ut.shape, lambda i, rs, cs, pos: (0, 0)),
            pl.BlockSpec(
                (1, NODE, block, cols), lambda i, rs, cs, pos: ((pos[0] - i + NX) % NX, 0, 0, 0)
            ),
        ],
        out_specs=pl.BlockSpec((rows // NX, cols), lambda i, rs, cs, pos: (i, 0)),
    )
    return pl.pallas_call(
        finish_kernel,
        out_shape=jax.ShapeDtypeStruct((rows, cols), BF),
        grid_spec=spec,
        interpret=INTERPRET,
    )(row_index, col_index, x.astype(jnp.int32).reshape(1), ancestor, ut, columns)


def corner_kernel(
    rs, cs, core, mine, other, diag, own, base, out, cross, kk, sem
):
    width = diag.shape[1]
    block = width // NODE
    for i in range(6):
        rows = slice((i % 3) * width, (i % 3 + 1) * width)
        cross[i] = jnp.where(core[0] == i // 3, mine[rows], other[rows]).astype(F32)
    c = {pair: cross.at[i] for i, pair in enumerate(PAIRS)}
    w10, w20, w21 = (own.at[:, i * width : (i + 1) * width] for i in range(3))

    def at(s, t):
        return kk.at[s * width : (s + 1) * width, t * width : (t + 1) * width]

    def diagonal(s, value):
        return (diag[s] - 0.5 * (value + value.T)).astype(BF)

    def keep(s, t, value):
        at(s, t)[...] = value.astype(BF)
        at(t, s)[...] = value.T.astype(BF)

    at(0, 0)[...] = diagonal(0, c[0, 0][...])
    keep(1, 0, -(c[1, 0][...] + mm(w10[...], at(0, 0)[...])))
    at(1, 1)[...] = diagonal(1, c[1, 1][...] + mm(w10[...], at(0, 1)[...]))
    keep(2, 0, -(c[2, 0][...] + mm(w20[...], at(0, 0)[...]) + mm(w21[...], at(1, 0)[...])))
    keep(2, 1, -(c[2, 1][...] + mm(w20[...], at(0, 1)[...]) + mm(w21[...], at(1, 1)[...])))
    at(2, 2)[...] = diagonal(
        2, c[2, 2][...] + mm(w20[...], at(0, 2)[...]) + mm(w21[...], at(1, 2)[...])
    )

    def each(act):
        def step(i, carry):
            row = rs[i]
            for j in range(NODE):
                col = cs[j]

                @pl.when((row >= 0) & (col >= 0))
                def _():
                    copy = pltpu.make_async_copy(
                        kk.at[pl.ds(row * block, block), pl.ds(col * block, block)],
                        out.at[pl.ds(i * block, block), pl.ds(j * block, block)],
                        sem,
                    )
                    act(copy)

            return carry

        lax.fori_loop(0, rs.shape[0], step, 0)

    each(lambda copy: copy.start())
    each(lambda copy: copy.wait())


def patch_corner(base, mine, other, diag_inverse, own, row_index, col_index, core):
    width = diag_inverse.shape[1]
    smem = pl.BlockSpec(memory_space=pltpu.SMEM)
    vmem = pl.BlockSpec(memory_space=pltpu.VMEM)
    anywhere = pl.BlockSpec(memory_space=pl.ANY)
    return pl.pallas_call(
        corner_kernel,
        out_shape=jax.ShapeDtypeStruct(base.shape, BF),
        in_specs=[smem, smem, smem, vmem, vmem, vmem, vmem, anywhere],
        out_specs=anywhere,
        scratch_shapes=[
            pltpu.VMEM((6, width, width), F32),
            pltpu.VMEM((S * width, S * width), BF),
            pltpu.SemaphoreType.DMA,
        ],
        input_output_aliases={7: 0},
        interpret=INTERPRET,
    )(row_index, col_index, core.astype(jnp.int32).reshape(1), mine, other, diag_inverse, own, base)


def contract(left, right, dims):
    return lax.dot_general(left, right, (dims, ((), ())), preferred_element_type=F32)


def mm(left, right):
    return contract(left, right, ((1,), (0,)))


def mmt(left, right):
    return contract(left, right, ((1,), (1,)))


def local(ancestor, panels, diag_inverse, supernode_blocks, row_lists):
    y, core, z, x = (lax.axis_index(name) for name in ("y", "core", "z", "x"))
    rows, cols = ancestor.shape
    block = cols // NODE
    width = NODE * block
    half = width // 2
    wl = panels.shape[1]
    row_blocks = rows // block
    group = 2 * y + core
    first_row = group * row_blocks
    first_col = (NX * z + x) * NODE
    k_list = supernode_blocks.reshape(-1)
    numbers = jnp.arange(S * NODE, dtype=jnp.int32) + 1

    def number_in(ids):
        return jnp.sum(jnp.where(ids[:, None] == k_list[None, :], numbers, 0), axis=1) - 1

    row_ids = first_row + jnp.arange(row_blocks, dtype=jnp.int32)
    row_index = number_in(row_ids)
    col_index = number_in(first_col + jnp.arange(NODE, dtype=jnp.int32))
    listed = jnp.any(row_ids[None, :, None] == row_lists[:, None, :], axis=2)

    with jax.named_scope("prepare"):
        first, second, own = prepare(panels, listed, k_list - first_row, block)

    with jax.named_scope("own_columns"):
        lane_half = 3 * half
        own_kept = by_core(core, own[:, :lane_half], own[:, lane_half:])
        own_sent = by_core(core, own[:, lane_half:], own[:, :lane_half])
        own_kept = own_kept + send(own_sent, "core", 1)
        own_sum = own_kept
        for step in range(1, NY):
            own_sum = own_sum + send(own_kept, "y", step)

    with jax.named_scope("gather_panels"):
        second_z = ring_gather(second, "z")
        first_x = ring_gather(jnp.concatenate([first, own_sum], axis=1), "x")
        first_zx = ring_gather(place(first_x, "x", x).reshape(NX * wl, -1), "z")
        second_z = place([p.reshape(2, wl, rows) for p in second_z], "z", z, 1)
        second_zx = ring_gather(second_z.reshape(2 * NZ * wl, rows), "x")

    with jax.named_scope("products"):
        active = jnp.where(
            (row_index < 0)[:, None, None], ancestor.reshape(row_blocks, block, cols), 0
        ).reshape(rows, cols)
        q0 = place([mm(part[:, :rows], active) for part in first_zx], "z", z)
        q12 = place(
            [mm(part, active).reshape(2, NZ, wl, cols) for part in second_zx], "x", x, 2
        )
        q0 = q0.reshape(width, cols)
        q12 = q12.reshape(2 * width, cols)

    with jax.named_scope("reduce_products"):
        low = jnp.concatenate([q0, q12[:half]], axis=0)
        high = q12[half:]
        q_chip = by_core(core, low, high) + send(by_core(core, high, low), "core", 1)
        q_mine = direct_scatter_sum(q_chip, "y", y, block, 1)
        q_other = send(q_mine, "core", 1)
        q_low = by_core(core, q_mine, q_other)
        q_high = by_core(core, q_other, q_mine)
        q = (
            q_low[:width],
            jnp.concatenate([q_low[width:], q_high[:half]], axis=0),
            q_high[half:],
        )
        own_mine = place([part[:, rows:] for part in first_zx], "z", z).reshape(width, lane_half)
        own_other = send(own_mine, "core", 1)
        own_all = jnp.concatenate(
            [by_core(core, own_mine, own_other), by_core(core, own_other, own_mine)], axis=1
        )
        w10, w20, w21 = (own_all[:, i * width : (i + 1) * width] for i in range(3))

    with jax.named_scope("update"):
        my_block = first_col + y
        outside = jnp.all(my_block != k_list)
        keep = [jnp.any(my_block == row_lists[s]) & outside for s in range(S)]
        u0 = jnp.where(keep[0], -q[0], 0.0).astype(BF)
        u1 = jnp.where(keep[1], -(q[1] + mm(w10, u0)), 0.0).astype(BF)
        u2 = jnp.where(keep[2], -(q[2] + mm(w20, u0) + mm(w21, u1)), 0.0).astype(BF)
        u = jnp.stack([u0, u1, u2])
        u_half = by_core(core, u[:, :half], u[:, half:])

    with jax.named_scope("turn"):
        pairs = []
        for fy in range(NY):
            for fc in range(NC):
                for fz in range(NZ):
                    target = ((fz // 2) * NC + fz % 2) * NZ + 2 * fy + fc
                    pairs.append(((fy * NC + fc) * NZ + fz, target))
        turned = lax.ppermute(u_half, ("y", "core", "z"), pairs)

    with jax.named_scope("inner"):
        lane = (NX * x + z // 2) * block

        def lanes(part):
            return lax.dynamic_slice_in_dim(part, lane, block, axis=1)

        p0 = place([lanes(part) for part in first_zx], "z", z).reshape(width, block)
        p12 = place(
            [lanes(part).reshape(2, NZ, wl, block) for part in second_zx], "x", x, 2
        ).reshape(2, width, block)
        p_rows = (p0, p12[0], p12[1])
        inner = [mmt(p_rows[s], turned[t]) for s, t in PAIRS]
        inner_a = jnp.concatenate(inner[:3], axis=0)
        inner_b = jnp.concatenate(inner[3:], axis=0)
        part = by_core(core, inner_a, inner_b) + send(by_core(core, inner_b, inner_a), "core", 1)
        part = direct_scatter_sum(part, "y", y, 3 * width // NY, 0)
        part = direct_scatter_sum(part, "x", x, 3 * width // (NY * NX), 0, F32)
        sent = part
        for step in (2, 4, 6):
            part = part + send(sent, "z", step)
        part = part.astype(BF)
        other = lax.ppermute(part, "z", [(i, i ^ 1) for i in range(NZ)])
        even = z % 2 == 0
        part = jnp.concatenate(
            [jnp.where(even, part, other), jnp.where(even, other, part)], axis=1
        )
        part = place(direct_gather(part, "x"), "x", x).reshape(-1, width)
        cross = place(ring_gather(part, "y"), "y", y).reshape(-1, width)
        cross_other = send(cross, "core", 1)

    with jax.named_scope("rows"):
        strips = direct_gather(u_half.reshape(3 * half, block), "y")
        strip = jnp.zeros((3 * half, cols), BF)
        for step, part in enumerate(strips):
            strip = lax.dynamic_update_slice(strip, part, (0, (y + step) % NY * block))
        strip = strip.reshape(S, half, cols)
        strip_other = send(strip, "core", 1)
        ut = jnp.concatenate(
            [by_core(core, strip, strip_other), by_core(core, strip_other, strip)], axis=1
        ).reshape(S * width, cols)

    with jax.named_scope("columns"):
        targets = (x + jnp.arange(NX, dtype=jnp.int32)) % NX
        wanted = (NX * group + targets[:, None]) * NODE + jnp.arange(NODE, dtype=jnp.int32)
        picked = pick(jnp.maximum(number_in(wanted.reshape(-1)), 0), ut, block)
        picked = picked.reshape(NX, NODE, block, cols)
        columns = []
        for step in range(NX):
            pairs = []
            for fy in range(NY):
                for fc in range(NC):
                    for fz in range(NZ):
                        for fx in range(NX):
                            target = ((fz // 2) * NC + fz % 2) * NZ + 2 * fy + fc
                            pairs.append(
                                (
                                    ((fy * NC + fc) * NZ + fz) * NX + fx,
                                    target * NX + (fx + step) % NX,
                                )
                            )
            columns.append(lax.ppermute(picked[step], ("y", "core", "z", "x"), pairs))
        columns = jnp.stack(columns)

    with jax.named_scope("finish"):
        base = finish(ancestor, ut, columns, row_index, col_index, x)
        return patch_corner(
            base, cross, cross_other, diag_inverse, own_all, row_index, col_index, core
        )


def solution(mesh):
    fine = Mesh(mesh.devices.reshape(NY, NC, NZ, NX), ("y", "core", "z", "x"))
    row, col = ("y", "core"), ("z", "x")
    in_specs = (P(row, col), P(None, col, row), P(), P(), P())
    return jax.shard_map(
        local, mesh=fine, in_specs=in_specs, out_specs=P(row, col), check_vma=False
    )
```

```python
import jax
import jax.numpy as jnp
from jax import lax
from jax.experimental import pallas as pl
from jax.experimental.pallas import tpu as pltpu
from jax.sharding import Mesh, PartitionSpec as P

S = 3
NODE = 4
NY, NC, NZ, NX = 4, 2, 8, 4
SIZES = {"y": NY, "core": NC, "z": NZ, "x": NX}
BF = jnp.bfloat16
F32 = jnp.float32
PAIRS = ((0, 0), (1, 0), (1, 1), (2, 0), (2, 1), (2, 2))
INTERPRET = False


def send(value, axis, step):
    size = SIZES[axis]
    return lax.ppermute(value, axis, [(i, (i + step) % size) for i in range(size)])


def ring_gather(value, axis, begun=None):
    size = SIZES[axis]
    found = [None] * size
    found[0] = value
    ahead = behind = value
    for step in range(1, size // 2):
        if step == 1 and begun is not None:
            behind, ahead = begun
        else:
            behind = send(behind, axis, 1)
            ahead = send(ahead, axis, -1)
        found[step] = ahead
        found[size - step] = behind
    half = value.shape[0] // 2
    found[size // 2] = jnp.concatenate(
        [send(behind[:half], axis, 1), send(ahead[half:], axis, -1)], axis=0
    )
    return found


def place(found, axis, position, dim=0):
    size = SIZES[axis]
    out = None
    for step, part in enumerate(found):
        part = jnp.expand_dims(part, dim)
        if out is None:
            shape = list(part.shape)
            shape[dim] = size
            out = jnp.zeros(shape, part.dtype)
        out = lax.dynamic_update_slice_in_dim(out, part, (position + step) % size, axis=dim)
    return out


def scatter_sum(pieces, axes, position):
    count = pieces.shape[0]
    got = lax.all_to_all(pieces.astype(BF), axes, 0, 0, tiled=True).astype(F32)
    ids = jnp.arange(count, dtype=jnp.int32)[:, None, None]
    return jnp.sum(jnp.where(ids == position, pieces, got), axis=0)


def gather(value, axes, count):
    spread = jnp.broadcast_to(value[None], (count, *value.shape))
    return lax.all_to_all(spread, axes, 0, 0, tiled=True)


def by_core(core, first, second):
    return jnp.where(core == 0, first, second)


def prepare_kernel(flags, at, p_ref, first_ref, second_ref, own_ref):
    wl = p_ref.shape[1]
    block = own_ref.shape[1] // (3 * NODE)
    row_blocks = p_ref.shape[2] // block
    for s in range(S):
        for b in range(row_blocks):
            span = slice(b * block, (b + 1) * block)
            value = p_ref[s, :, span]
            value = jnp.where(flags[s * row_blocks + b] > 0, value, jnp.zeros_like(value))
            if s == 0:
                first_ref[:, span] = value
            else:
                second_ref[(s - 1) * wl : s * wl, span] = value
    for pair, (s, t) in enumerate(((1, 0), (2, 0), (2, 1))):
        for k in range(NODE):
            index = at[t * NODE + k]
            inside = (index >= 0) & (index < row_blocks)
            start = pl.multiple_of(jnp.where(inside, index, 0) * block, block)
            value = p_ref[s, :, pl.ds(start, block)]
            value = jnp.where(inside, value, jnp.zeros_like(value))
            own_ref[:, (pair * NODE + k) * block : (pair * NODE + k + 1) * block] = value


def prepare(panels, listed, at, block):
    _, wl, rows = panels.shape
    return pl.pallas_call(
        prepare_kernel,
        out_shape=(
            jax.ShapeDtypeStruct((wl, rows), BF),
            jax.ShapeDtypeStruct((2 * wl, rows), BF),
            jax.ShapeDtypeStruct((wl, 3 * NODE * block), BF),
        ),
        in_specs=[
            pl.BlockSpec(memory_space=pltpu.SMEM),
            pl.BlockSpec(memory_space=pltpu.SMEM),
            pl.BlockSpec(memory_space=pltpu.VMEM),
        ],
        interpret=INTERPRET,
    )(listed.astype(jnp.int32).reshape(-1), at, panels)


def pick_kernel(index, ut_ref, out_ref):
    block = ut_ref.shape[2]

    def step(i, carry):
        start = pl.multiple_of(index[i] * block, block)
        for q in range(NODE):
            out_ref[i, q] = ut_ref[q, pl.ds(start, block), :]
        return carry

    lax.fori_loop(0, out_ref.shape[0], step, 0)


def pick(index, ut):
    block = ut.shape[2]
    return pl.pallas_call(
        pick_kernel,
        out_shape=jax.ShapeDtypeStruct((index.shape[0], NODE, block, block), BF),
        in_specs=[
            pl.BlockSpec(memory_space=pltpu.SMEM),
            pl.BlockSpec(memory_space=pltpu.VMEM),
        ],
        interpret=INTERPRET,
    )(index, ut)


def strips_kernel(rs, cs, slots, pos, ut, near, far, base, out, buffer, sem_col, sem_row):
    block = ut.shape[2]
    row_blocks = rs.shape[0]

    def column(j):
        return pltpu.make_async_copy(
            buffer.at[j], out.at[:, pl.ds(j * block, block)], sem_col.at[j]
        )

    for j in range(NODE):
        slot = slots[j]

        def fill(i, carry, j=j, slot=slot):
            step = (pos[0] - i + NX) % NX
            for q in range(NODE):
                at = pl.multiple_of((i * NODE + q) * block, block)
                tile = jnp.where(
                    slot < 2,
                    near[step, jnp.minimum(slot, 1), q],
                    far[i, jnp.maximum(slot - 2, 0), q],
                )
                buffer[j, pl.ds(at, block), :] = tile.astype(F32).T.astype(BF)
            return carry

        @pl.when(cs[j] >= 0)
        def _(j=j, fill=fill):
            lax.fori_loop(0, NX, fill, 0)
            column(j).start()

    for j in range(NODE):

        @pl.when(cs[j] >= 0)
        def _(j=j):
            column(j).wait()

    def each(act):
        def step(i, carry):
            row = rs[i]

            @pl.when(row >= 0)
            def _():
                for j in range(NODE):
                    act(
                        pltpu.make_async_copy(
                            ut.at[j, pl.ds(row * block, block), :],
                            out.at[pl.ds(i * block, block), pl.ds(j * block, block)],
                            sem_row,
                        )
                    )

            return carry

        lax.fori_loop(0, row_blocks, step, 0)

    each(lambda copy: copy.start())
    each(lambda copy: copy.wait())


def patch_strips(ancestor, ut, near, far, row_index, col_index, slots, x):
    rows, cols = ancestor.shape
    block = cols // NODE
    smem = pl.BlockSpec(memory_space=pltpu.SMEM)
    vmem = pl.BlockSpec(memory_space=pltpu.VMEM)
    anywhere = pl.BlockSpec(memory_space=pl.ANY)
    return pl.pallas_call(
        strips_kernel,
        out_shape=jax.ShapeDtypeStruct((rows, cols), BF),
        in_specs=[smem, smem, smem, smem, vmem, vmem, vmem, anywhere],
        out_specs=anywhere,
        scratch_shapes=[
            pltpu.VMEM((NODE, rows, block), BF),
            pltpu.SemaphoreType.DMA((NODE,)),
            pltpu.SemaphoreType.DMA,
        ],
        input_output_aliases={7: 0},
        interpret=INTERPRET,
    )(row_index, col_index, slots, x.astype(jnp.int32).reshape(1), ut, near, far, ancestor)


def corner_kernel(
    rs, cs, core, mine, other, diag, own, base, out, cross, kk, sem
):
    width = diag.shape[1]
    block = width // NODE
    for i in range(6):
        rows = slice((i % 3) * width, (i % 3 + 1) * width)
        cross[i] = jnp.where(core[0] == i // 3, mine[rows], other[rows]).astype(F32)
    c = {pair: cross.at[i] for i, pair in enumerate(PAIRS)}
    w10, w20, w21 = (own.at[:, i * width : (i + 1) * width] for i in range(3))

    def at(s, t):
        return kk.at[s * width : (s + 1) * width, t * width : (t + 1) * width]

    def diagonal(s, value):
        return (diag[s] - 0.5 * (value + value.T)).astype(BF)

    def keep(s, t, value):
        at(s, t)[...] = value.astype(BF)
        at(t, s)[...] = value.T.astype(BF)

    at(0, 0)[...] = diagonal(0, c[0, 0][...])
    keep(1, 0, -(c[1, 0][...] + mm(w10[...], at(0, 0)[...])))
    at(1, 1)[...] = diagonal(1, c[1, 1][...] + mm(w10[...], at(0, 1)[...]))
    keep(2, 0, -(c[2, 0][...] + mm(w20[...], at(0, 0)[...]) + mm(w21[...], at(1, 0)[...])))
    keep(2, 1, -(c[2, 1][...] + mm(w20[...], at(0, 1)[...]) + mm(w21[...], at(1, 1)[...])))
    at(2, 2)[...] = diagonal(
        2, c[2, 2][...] + mm(w20[...], at(0, 2)[...]) + mm(w21[...], at(1, 2)[...])
    )

    def each(act):
        def step(i, carry):
            row = rs[i]
            for j in range(NODE):
                col = cs[j]

                @pl.when((row >= 0) & (col >= 0))
                def _():
                    copy = pltpu.make_async_copy(
                        kk.at[pl.ds(row * block, block), pl.ds(col * block, block)],
                        out.at[pl.ds(i * block, block), pl.ds(j * block, block)],
                        sem,
                    )
                    act(copy)

            return carry

        lax.fori_loop(0, rs.shape[0], step, 0)

    each(lambda copy: copy.start())
    each(lambda copy: copy.wait())


def patch_corner(base, mine, other, diag_inverse, own, row_index, col_index, core):
    width = diag_inverse.shape[1]
    smem = pl.BlockSpec(memory_space=pltpu.SMEM)
    vmem = pl.BlockSpec(memory_space=pltpu.VMEM)
    anywhere = pl.BlockSpec(memory_space=pl.ANY)
    return pl.pallas_call(
        corner_kernel,
        out_shape=jax.ShapeDtypeStruct(base.shape, BF),
        in_specs=[smem, smem, smem, vmem, vmem, vmem, vmem, anywhere],
        out_specs=anywhere,
        scratch_shapes=[
            pltpu.VMEM((6, width, width), F32),
            pltpu.VMEM((S * width, S * width), BF),
            pltpu.SemaphoreType.DMA,
        ],
        input_output_aliases={7: 0},
        interpret=INTERPRET,
    )(row_index, col_index, core.astype(jnp.int32).reshape(1), mine, other, diag_inverse, own, base)


def contract(left, right, dims):
    return lax.dot_general(left, right, (dims, ((), ())), preferred_element_type=F32)


def mm(left, right):
    return contract(left, right, ((1,), (0,)))


def mmt(left, right):
    return contract(left, right, ((1,), (1,)))


def local(ancestor, panels, diag_inverse, supernode_blocks, row_lists):
    y, core, z, x = (lax.axis_index(name) for name in ("y", "core", "z", "x"))
    rows, cols = ancestor.shape
    block = cols // NODE
    width = NODE * block
    half = width // 2
    wl = panels.shape[1]
    row_blocks = rows // block
    group = 2 * y + core
    first_row = group * row_blocks
    first_col = (NX * z + x) * NODE
    k_list = supernode_blocks.reshape(-1)
    numbers = jnp.arange(S * NODE, dtype=jnp.int32) + 1

    def number_in(ids):
        return jnp.sum(jnp.where(ids[:, None] == k_list[None, :], numbers, 0), axis=1) - 1

    row_ids = first_row + jnp.arange(row_blocks, dtype=jnp.int32)
    row_index = number_in(row_ids)
    col_index = number_in(first_col + jnp.arange(NODE, dtype=jnp.int32))
    listed = jnp.any(row_ids[None, :, None] == row_lists[:, None, :], axis=2)

    with jax.named_scope("prepare"):
        first, second, own = prepare(panels, listed, k_list - first_row, block)

    with jax.named_scope("gather_panels"):
        lane_half = 3 * half
        own_kept = by_core(core, own[:, :lane_half], own[:, lane_half:])
        own_sent = by_core(core, own[:, lane_half:], own[:, :lane_half])
        back1, front1, own_got = lax.optimization_barrier(
            (send(second, "z", 1), send(second, "z", -1), send(own_sent, "core", 1))
        )
        own_kept = own_kept + own_got
        back2, front2, *own_parts = lax.optimization_barrier(
            (
                send(back1, "z", 1),
                send(front1, "z", -1),
                *[send(own_kept, "y", step) for step in range(1, NY)],
            )
        )
        for part in own_parts:
            own_kept = own_kept + part
        first = jnp.concatenate([first, own_kept], axis=1)
        back3, front3, *first_x = lax.optimization_barrier(
            (
                send(back2, "z", 1),
                send(front2, "z", -1),
                send(first, "x", -1),
                send(first, "x", 2),
                send(first, "x", 1),
            )
        )
        first_x = place([first, *first_x], "x", x).reshape(NX * wl, -1)
        back4, front4, first_back, first_front = lax.optimization_barrier(
            (
                send(back3[:wl], "z", 1),
                send(front3[wl:], "z", -1),
                send(first_x, "z", 1),
                send(first_x, "z", -1),
            )
        )
        middle = jnp.concatenate([back4, front4], axis=0)
        second_z = [second, front1, front2, front3, middle, back3, back2, back1]
        second_z = place([p.reshape(2, wl, rows) for p in second_z], "z", z, 1)
        second_zx = ring_gather(second_z.reshape(2 * NZ * wl, rows), "x")
        first_zx = ring_gather(first_x, "z", (first_back, first_front))

    with jax.named_scope("products"):
        active = jnp.where(
            (row_index < 0)[:, None, None], ancestor.reshape(row_blocks, block, cols), 0
        ).reshape(rows, cols)
        q0 = place([mm(part[:, :rows], active) for part in first_zx], "z", z)
        q12 = place(
            [mm(part, active).reshape(2, NZ, wl, cols) for part in second_zx], "x", x, 2
        )
        q0 = q0.reshape(width, cols)
        q12 = q12.reshape(2 * width, cols)

    with jax.named_scope("reduce_products"):
        low = jnp.concatenate([q0, q12[:half]], axis=0)
        high = q12[half:]
        q_chip = by_core(core, low, high) + send(by_core(core, high, low), "core", 1)
        q_mine = scatter_sum(q_chip.reshape(-1, NY, block).transpose(1, 0, 2), ("y",), y)
        q_other = send(q_mine, "core", 1)
        q_low = by_core(core, q_mine, q_other)
        q_high = by_core(core, q_other, q_mine)
        q = (
            q_low[:width],
            jnp.concatenate([q_low[width:], q_high[:half]], axis=0),
            q_high[half:],
        )
        own_mine = place([part[:, rows:] for part in first_zx], "z", z).reshape(width, lane_half)
        own_other = send(own_mine, "core", 1)
        own_all = jnp.concatenate(
            [by_core(core, own_mine, own_other), by_core(core, own_other, own_mine)], axis=1
        )
        w10, w20, w21 = (own_all[:, i * width : (i + 1) * width] for i in range(3))

    with jax.named_scope("update"):
        my_block = first_col + y
        outside = jnp.all(my_block != k_list)
        keep = [jnp.any(my_block == row_lists[s]) & outside for s in range(S)]
        u0 = jnp.where(keep[0], -q[0], 0.0).astype(BF)
        u1 = jnp.where(keep[1], -(q[1] + mm(w10, u0)), 0.0).astype(BF)
        u2 = jnp.where(keep[2], -(q[2] + mm(w20, u0) + mm(w21, u1)), 0.0).astype(BF)
        u = jnp.stack([u0, u1, u2])
        u_half = by_core(core, u[:, :half], u[:, half:])

    with jax.named_scope("turn"):
        pairs = []
        for fy in range(NY):
            for fc in range(NC):
                for fz in range(NZ):
                    pair_z = (fy + fz // 2 + (fz < 2)) % NY
                    target = ((fz // 2) * NC + fz % 2) * NZ + 2 * pair_z + fc
                    pairs.append(((fy * NC + fc) * NZ + fz, target))
        turned = lax.ppermute(u_half, ("y", "core", "z"), pairs)
        strip = gather(u_half.reshape(3 * half, block), ("y",), NY)
        turned, strip = lax.optimization_barrier((turned, strip))

    with jax.named_scope("inner"):
        lane = (NX * x + (z // 2 - y - (y == 0)) % NY) * block

        def lanes(part):
            return lax.dynamic_slice_in_dim(part, lane, block, axis=1)

        p0 = place([lanes(part) for part in first_zx], "z", z).reshape(width, block)
        p12 = place(
            [lanes(part).reshape(2, NZ, wl, block) for part in second_zx], "x", x, 2
        ).reshape(2, width, block)
        p_rows = (p0, p12[0], p12[1])
        inner = [mmt(p_rows[s], turned[t]) for s, t in PAIRS]
        inner_a = jnp.concatenate(inner[:3], axis=0)
        inner_b = jnp.concatenate(inner[3:], axis=0)
        got = send(by_core(core, inner_b, inner_a), "core", 1)
        strip_other = send(strip, "core", 1)
        got, strip_other = lax.optimization_barrier((got, strip_other))
        part = by_core(core, inner_a, inner_b) + got

    with jax.named_scope("columns"):
        strip = strip.reshape(NY, S, 1, half, block)
        strip_other = strip_other.reshape(NY, S, 1, half, block)
        ut = jnp.concatenate(
            [by_core(core, strip, strip_other), by_core(core, strip_other, strip)], axis=2
        ).reshape(NY, S * width, block)

        def turn_z(fy, fc, fz, step):
            return (fz + 2 * fy + fc + 2 * step + (1 if fz == 0 else 0)) % NZ

        def slots_of(z_at, x_at):
            found = number_in((NX * z_at + x_at) * NODE + jnp.arange(NODE, dtype=jnp.int32))
            rank = jnp.cumsum((found >= 0).astype(jnp.int32)) - 1
            ids = jnp.arange(NODE, dtype=jnp.int32)[:, None]
            hit = (found >= 0)[None, :] & (rank[None, :] == ids)
            return jnp.sum(jnp.where(hit, found[None, :], 0), axis=1), rank

        shift = z + group + jnp.where(z == 0, 1, 0)
        near_index = jnp.concatenate(
            [slots_of((shift + 2 * step) % NZ, (x + step) % NX)[0][:2] for step in range(NX)]
        )
        picked = pick(near_index, ut).reshape(NX, 2, NODE, block, block)
        near = []
        for step in range(NX):
            pairs = []
            for fy in range(NY):
                for fc in range(NC):
                    for fz in range(NZ):
                        for fx in range(NX):
                            target = ((fz // 2) * NC + fz % 2) * NZ + turn_z(fy, fc, fz, step)
                            pairs.append(
                                (
                                    ((fy * NC + fc) * NZ + fz) * NX + fx,
                                    target * NX + (fx + step) % NX,
                                )
                            )
            near.append(lax.ppermute(picked[step], ("y", "core", "z", "x"), pairs))
        near = jnp.stack(near)

        def more(ut):
            index = jnp.concatenate([slots_of(shift % NZ, at)[0][2:] for at in range(NX)])
            value = pick(index, ut)
            pairs = []
            for fy in range(NY):
                for fc in range(NC):
                    for fz in range(NZ):
                        target = ((fz // 2) * NC + fz % 2) * NZ + turn_z(fy, fc, fz, 0)
                        pairs.append(((fy * NC + fc) * NZ + fz, target))
            value = lax.ppermute(value, ("y", "core", "z"), pairs)
            value = value.reshape(NX, 2 * NODE, block, block)
            value = lax.all_to_all(value, ("x",), 0, 0, tiled=True)
            return value.reshape(NX, 2, NODE, block, block)

        def none(ut):
            return jnp.zeros((NX, 2, NODE, block, block), BF)

        owners = k_list // NODE
        crowd = jnp.max(jnp.sum((owners[:, None] == owners[None, :]).astype(jnp.int32), axis=1))
        far = lax.cond(crowd > 2, more, none, ut)
        my_slots = slots_of(z, x)[1]

    with jax.named_scope("inner"):
        pieces = part.reshape(NY * NX, 3 * width // (NY * NX), half)
        part = scatter_sum(pieces, ("y", "x"), y * NX + x)
        sent = part
        for step in (2, 4, 6):
            part = part + send(sent, "z", step)
        part = part.astype(BF)
        other = lax.ppermute(part, "z", [(i, i ^ 1) for i in range(NZ)])
        even = z % 2 == 0
        part = jnp.concatenate(
            [jnp.where(even, part, other), jnp.where(even, other, part)], axis=1
        )
        cross = gather(part, ("y", "x"), NY * NX).reshape(3 * width, width)
        cross_other = send(cross, "core", 1)

    with jax.named_scope("finish"):
        base = patch_strips(ancestor, ut, near, far, row_index, col_index, my_slots, x)
        return patch_corner(
            base, cross, cross_other, diag_inverse, own_all, row_index, col_index, core
        )


def solution(mesh):
    fine = Mesh(mesh.devices.reshape(NY, NC, NZ, NX), ("y", "core", "z", "x"))
    row, col = ("y", "core"), ("z", "x")
    in_specs = (P(row, col), P(None, col, row), P(), P(), P())
    return jax.shard_map(
        local, mesh=fine, in_specs=in_specs, out_specs=P(row, col), check_vma=False
    )
```

```python
import jax
import jax.numpy as jnp
from jax import lax
from jax.experimental import pallas as pl
from jax.experimental.pallas import tpu as pltpu
from jax.sharding import Mesh, PartitionSpec as P

S = 3
NODE = 4
NY, NC, NZ, NX = 4, 2, 8, 4
SIZES = {"y": NY, "core": NC, "z": NZ, "x": NX}
BF = jnp.bfloat16
F32 = jnp.float32
PAIRS = ((0, 0), (1, 0), (1, 1), (2, 0), (2, 1), (2, 2))
INTERPRET = False


def send(value, axis, step):
    size = SIZES[axis]
    return lax.ppermute(value, axis, [(i, (i + step) % size) for i in range(size)])


def ring_gather(value, axis, begun=None):
    size = SIZES[axis]
    found = [None] * size
    found[0] = value
    ahead = behind = value
    for step in range(1, size // 2):
        if step == 1 and begun is not None:
            behind, ahead = begun
        else:
            behind = send(behind, axis, 1)
            ahead = send(ahead, axis, -1)
        found[step] = ahead
        found[size - step] = behind
    half = value.shape[0] // 2
    found[size // 2] = jnp.concatenate(
        [send(behind[:half], axis, 1), send(ahead[half:], axis, -1)], axis=0
    )
    return found


def place(found, axis, position, dim=0):
    size = SIZES[axis]
    out = None
    for step, part in enumerate(found):
        part = jnp.expand_dims(part, dim)
        if out is None:
            shape = list(part.shape)
            shape[dim] = size
            out = jnp.zeros(shape, part.dtype)
        out = lax.dynamic_update_slice_in_dim(out, part, (position + step) % size, axis=dim)
    return out


def scatter_sum(pieces, axes, position):
    count = pieces.shape[0]
    got = lax.all_to_all(pieces.astype(BF), axes, 0, 0, tiled=True).astype(F32)
    ids = jnp.arange(count, dtype=jnp.int32)[:, None, None]
    return jnp.sum(jnp.where(ids == position, pieces, got), axis=0)


def gather(value, axes, count):
    spread = jnp.broadcast_to(value[None], (count, *value.shape))
    return lax.all_to_all(spread, axes, 0, 0, tiled=True)


def by_core(core, first, second):
    return jnp.where(core == 0, first, second)


def prepare_kernel(flags, at, p_ref, first_ref, second_ref, own_ref):
    wl = p_ref.shape[1]
    block = own_ref.shape[1] // (3 * NODE)
    row_blocks = p_ref.shape[2] // block
    for s in range(S):
        for b in range(row_blocks):
            span = slice(b * block, (b + 1) * block)
            value = p_ref[s, :, span]
            value = jnp.where(flags[s * row_blocks + b] > 0, value, jnp.zeros_like(value))
            if s == 0:
                first_ref[:, span] = value
            else:
                second_ref[(s - 1) * wl : s * wl, span] = value
    for pair, (s, t) in enumerate(((1, 0), (2, 0), (2, 1))):
        for k in range(NODE):
            index = at[t * NODE + k]
            inside = (index >= 0) & (index < row_blocks)
            start = pl.multiple_of(jnp.where(inside, index, 0) * block, block)
            value = p_ref[s, :, pl.ds(start, block)]
            value = jnp.where(inside, value, jnp.zeros_like(value))
            own_ref[:, (pair * NODE + k) * block : (pair * NODE + k + 1) * block] = value


def prepare(panels, listed, at, block):
    _, wl, rows = panels.shape
    return pl.pallas_call(
        prepare_kernel,
        out_shape=(
            jax.ShapeDtypeStruct((wl, rows), BF),
            jax.ShapeDtypeStruct((2 * wl, rows), BF),
            jax.ShapeDtypeStruct((wl, 3 * NODE * block), BF),
        ),
        in_specs=[
            pl.BlockSpec(memory_space=pltpu.SMEM),
            pl.BlockSpec(memory_space=pltpu.SMEM),
            pl.BlockSpec(memory_space=pltpu.VMEM),
        ],
        interpret=INTERPRET,
    )(listed.astype(jnp.int32).reshape(-1), at, panels)


def extract_kernel(pos, *refs):
    first, second = refs[:NZ], refs[NZ : NZ + NX]
    p0, p12, own, sem = refs[NZ + NX :]
    rows = second[0].shape[3]
    block = p0.shape[2]
    lane = pl.multiple_of(pos[2], block)
    copies = []
    for d, ref in enumerate(first):
        at = (pos[0] + d) % NZ
        copies.append((ref.at[:, pl.ds(lane, block)], p0.at[at]))
        copies.append((ref.at[:, pl.ds(rows, own.shape[2])], own.at[at]))
    for d, ref in enumerate(second):
        at = (pos[1] + d) % NX
        copies.append((ref.at[:, :, :, pl.ds(lane, block)], p12.at[:, :, at]))
    copies = [pltpu.make_async_copy(*pair, sem.at[i]) for i, pair in enumerate(copies)]
    for copy in copies:
        copy.start()
    for copy in copies:
        copy.wait()


def extract(first_zx, second_zx, z, x, lane, block, wl):
    second_zx = [part.reshape(2, NZ, wl, -1) for part in second_zx]
    extra = first_zx[0].shape[1] - second_zx[0].shape[3]
    anywhere = pl.BlockSpec(memory_space=pl.ANY)
    p0, p12, own = pl.pallas_call(
        extract_kernel,
        out_shape=(
            jax.ShapeDtypeStruct((NZ, NX * wl, block), BF),
            jax.ShapeDtypeStruct((2, NZ, NX, wl, block), BF),
            jax.ShapeDtypeStruct((NZ, NX * wl, extra), BF),
        ),
        in_specs=[pl.BlockSpec(memory_space=pltpu.SMEM), *[anywhere] * (NZ + NX)],
        out_specs=(anywhere, anywhere, anywhere),
        scratch_shapes=[pltpu.SemaphoreType.DMA((2 * NZ + NX,))],
        interpret=INTERPRET,
    )(jnp.stack([z, x, lane]).astype(jnp.int32), *first_zx, *second_zx)
    width = NZ * NX * wl
    return p0.reshape(width, block), p12.reshape(2, width, block), own.reshape(width, extra)


def pick_kernel(index, ut_ref, out_ref):
    block = ut_ref.shape[2]

    def step(i, carry):
        start = pl.multiple_of(index[i] * block, block)
        for q in range(NODE):
            out_ref[i, q] = ut_ref[q, pl.ds(start, block), :]
        return carry

    lax.fori_loop(0, out_ref.shape[0], step, 0)


def pick(index, ut):
    block = ut.shape[2]
    return pl.pallas_call(
        pick_kernel,
        out_shape=jax.ShapeDtypeStruct((index.shape[0], NODE, block, block), BF),
        in_specs=[
            pl.BlockSpec(memory_space=pltpu.SMEM),
            pl.BlockSpec(memory_space=pltpu.VMEM),
        ],
        interpret=INTERPRET,
    )(index, ut)


def strips_kernel(rs, cs, slots, pos, ut, near, far, base, out, buffer, sem_col, sem_row):
    block = ut.shape[2]
    row_blocks = rs.shape[0]

    def column(j):
        return pltpu.make_async_copy(
            buffer.at[j], out.at[:, pl.ds(j * block, block)], sem_col.at[j]
        )

    for j in range(NODE):
        slot = slots[j]

        def fill(i, carry, j=j, slot=slot):
            step = (pos[0] - i + NX) % NX
            for q in range(NODE):
                at = pl.multiple_of((i * NODE + q) * block, block)
                tile = jnp.where(
                    slot < 2,
                    near[step, jnp.minimum(slot, 1), q],
                    far[i, jnp.maximum(slot - 2, 0), q],
                )
                buffer[j, pl.ds(at, block), :] = tile.astype(F32).T.astype(BF)
            return carry

        @pl.when(cs[j] >= 0)
        def _(j=j, fill=fill):
            lax.fori_loop(0, NX, fill, 0)
            column(j).start()

    for j in range(NODE):

        @pl.when(cs[j] >= 0)
        def _(j=j):
            column(j).wait()

    def each(act):
        def step(i, carry):
            row = rs[i]

            @pl.when(row >= 0)
            def _():
                for j in range(NODE):
                    act(
                        pltpu.make_async_copy(
                            ut.at[j, pl.ds(row * block, block), :],
                            out.at[pl.ds(i * block, block), pl.ds(j * block, block)],
                            sem_row,
                        )
                    )

            return carry

        lax.fori_loop(0, row_blocks, step, 0)

    each(lambda copy: copy.start())
    each(lambda copy: copy.wait())


def patch_strips(ancestor, ut, near, far, row_index, col_index, slots, x):
    rows, cols = ancestor.shape
    block = cols // NODE
    smem = pl.BlockSpec(memory_space=pltpu.SMEM)
    vmem = pl.BlockSpec(memory_space=pltpu.VMEM)
    anywhere = pl.BlockSpec(memory_space=pl.ANY)
    return pl.pallas_call(
        strips_kernel,
        out_shape=jax.ShapeDtypeStruct((rows, cols), BF),
        in_specs=[smem, smem, smem, smem, vmem, vmem, vmem, anywhere],
        out_specs=anywhere,
        scratch_shapes=[
            pltpu.VMEM((NODE, rows, block), BF),
            pltpu.SemaphoreType.DMA((NODE,)),
            pltpu.SemaphoreType.DMA,
        ],
        input_output_aliases={7: 0},
        interpret=INTERPRET,
    )(row_index, col_index, slots, x.astype(jnp.int32).reshape(1), ut, near, far, ancestor)


def corner_kernel(
    rs, cs, core, mine, other, diag, own, base, out, cross, kk, sem
):
    width = diag.shape[1]
    block = width // NODE
    for i in range(6):
        rows = slice((i % 3) * width, (i % 3 + 1) * width)
        cross[i] = jnp.where(core[0] == i // 3, mine[rows], other[rows]).astype(F32)
    c = {pair: cross.at[i] for i, pair in enumerate(PAIRS)}
    w10, w20, w21 = (own.at[:, i * width : (i + 1) * width] for i in range(3))

    def at(s, t):
        return kk.at[s * width : (s + 1) * width, t * width : (t + 1) * width]

    def diagonal(s, value):
        return (diag[s] - 0.5 * (value + value.T)).astype(BF)

    def keep(s, t, value):
        at(s, t)[...] = value.astype(BF)
        at(t, s)[...] = value.T.astype(BF)

    at(0, 0)[...] = diagonal(0, c[0, 0][...])
    keep(1, 0, -(c[1, 0][...] + mm(w10[...], at(0, 0)[...])))
    at(1, 1)[...] = diagonal(1, c[1, 1][...] + mm(w10[...], at(0, 1)[...]))
    keep(2, 0, -(c[2, 0][...] + mm(w20[...], at(0, 0)[...]) + mm(w21[...], at(1, 0)[...])))
    keep(2, 1, -(c[2, 1][...] + mm(w20[...], at(0, 1)[...]) + mm(w21[...], at(1, 1)[...])))
    at(2, 2)[...] = diagonal(
        2, c[2, 2][...] + mm(w20[...], at(0, 2)[...]) + mm(w21[...], at(1, 2)[...])
    )

    def each(act):
        def step(i, carry):
            row = rs[i]
            for j in range(NODE):
                col = cs[j]

                @pl.when((row >= 0) & (col >= 0))
                def _():
                    copy = pltpu.make_async_copy(
                        kk.at[pl.ds(row * block, block), pl.ds(col * block, block)],
                        out.at[pl.ds(i * block, block), pl.ds(j * block, block)],
                        sem,
                    )
                    act(copy)

            return carry

        lax.fori_loop(0, rs.shape[0], step, 0)

    each(lambda copy: copy.start())
    each(lambda copy: copy.wait())


def patch_corner(base, mine, other, diag_inverse, own, row_index, col_index, core):
    width = diag_inverse.shape[1]
    smem = pl.BlockSpec(memory_space=pltpu.SMEM)
    vmem = pl.BlockSpec(memory_space=pltpu.VMEM)
    anywhere = pl.BlockSpec(memory_space=pl.ANY)
    return pl.pallas_call(
        corner_kernel,
        out_shape=jax.ShapeDtypeStruct(base.shape, BF),
        in_specs=[smem, smem, smem, vmem, vmem, vmem, vmem, anywhere],
        out_specs=anywhere,
        scratch_shapes=[
            pltpu.VMEM((6, width, width), F32),
            pltpu.VMEM((S * width, S * width), BF),
            pltpu.SemaphoreType.DMA,
        ],
        input_output_aliases={7: 0},
        interpret=INTERPRET,
    )(row_index, col_index, core.astype(jnp.int32).reshape(1), mine, other, diag_inverse, own, base)


def contract(left, right, dims):
    return lax.dot_general(left, right, (dims, ((), ())), preferred_element_type=F32)


def mm(left, right):
    return contract(left, right, ((1,), (0,)))


def mmt(left, right):
    return contract(left, right, ((1,), (1,)))


def update_all(ancestor, panels, diag_inverse, supernode_blocks, row_lists):
    y, core, z, x = (lax.axis_index(name) for name in ("y", "core", "z", "x"))
    rows, cols = ancestor.shape
    block = cols // NODE
    width = NODE * block
    half = width // 2
    wl = panels.shape[1]
    row_blocks = rows // block
    group = 2 * y + core
    first_row = group * row_blocks
    first_col = (NX * z + x) * NODE
    k_list = supernode_blocks.reshape(-1)
    numbers = jnp.arange(S * NODE, dtype=jnp.int32) + 1

    def number_in(ids):
        return jnp.sum(jnp.where(ids[:, None] == k_list[None, :], numbers, 0), axis=1) - 1

    row_ids = first_row + jnp.arange(row_blocks, dtype=jnp.int32)
    row_index = number_in(row_ids)
    col_index = number_in(first_col + jnp.arange(NODE, dtype=jnp.int32))
    listed = jnp.any(row_ids[None, :, None] == row_lists[:, None, :], axis=2)

    first, second, own = prepare(panels, listed, k_list - first_row, block)

    lane_half = 3 * half
    own_kept = by_core(core, own[:, :lane_half], own[:, lane_half:])
    own_sent = by_core(core, own[:, lane_half:], own[:, :lane_half])
    second_z = gather(second.reshape(2, wl, rows), ("z",), NZ)
    own_kept = own_kept + send(own_sent, "core", 1)
    own_sum = own_kept
    for step in range(1, NY):
        own_sum = own_sum + send(own_kept, "y", step)
    first = jnp.concatenate([first, own_sum], axis=1)
    first_x = [first, send(first, "x", -1), send(first, "x", 2), send(first, "x", 1)]
    first_x = place(first_x, "x", x).reshape(NX * wl, -1)
    second_z, *begun = lax.optimization_barrier(
        (second_z, send(first_x, "z", 1), send(first_x, "z", -1))
    )
    first_zx = ring_gather(first_x, "z", begun)
    second_z = second_z.transpose(1, 0, 2, 3).reshape(2 * NZ * wl, rows)
    second_zx = ring_gather(second_z, "x")

    active = jnp.where(
        (row_index < 0)[:, None, None], ancestor.reshape(row_blocks, block, cols), 0
    ).reshape(rows, cols)
    q0 = place([mm(part[:, :rows], active) for part in first_zx], "z", z)
    q12 = place(
        [mm(part, active).reshape(2, NZ, wl, cols) for part in second_zx], "x", x, 2
    )
    q0 = q0.reshape(width, cols)
    q12 = q12.reshape(2 * width, cols)

    low = jnp.concatenate([q0, q12[:half]], axis=0)
    high = q12[half:]
    q_chip = by_core(core, low, high) + send(by_core(core, high, low), "core", 1)

    def strip_of(owner):
        return lax.dynamic_slice_in_dim(q_chip, owner * block, block, axis=1)

    q_mine = strip_of(y)
    for step in range(1, NY):
        q_mine = q_mine + send(strip_of((y + step) % NY).astype(BF), "y", step).astype(F32)
    q_other = send(q_mine, "core", 1)
    q_low = by_core(core, q_mine, q_other)
    q_high = by_core(core, q_other, q_mine)
    q = (
        q_low[:width],
        jnp.concatenate([q_low[width:], q_high[:half]], axis=0),
        q_high[half:],
    )
    lane = (NX * x + (z // 2 - y - (y == 0)) % NY) * block
    p0, p12, own_mine = extract(first_zx, second_zx, z, x, lane, block, wl)
    p_rows = (p0, p12[0], p12[1])
    own_other = send(own_mine, "core", 1)
    own_all = jnp.concatenate(
        [by_core(core, own_mine, own_other), by_core(core, own_other, own_mine)], axis=1
    )
    w10, w20, w21 = (own_all[:, i * width : (i + 1) * width] for i in range(3))

    my_block = first_col + y
    outside = jnp.all(my_block != k_list)
    keep = [jnp.any(my_block == row_lists[s]) & outside for s in range(S)]
    u0 = jnp.where(keep[0], -q[0], 0.0).astype(BF)
    u1 = jnp.where(keep[1], -(q[1] + mm(w10, u0)), 0.0).astype(BF)
    u2 = jnp.where(keep[2], -(q[2] + mm(w20, u0) + mm(w21, u1)), 0.0).astype(BF)
    u = jnp.stack([u0, u1, u2])
    u_half = by_core(core, u[:, :half], u[:, half:])

    pairs = []
    for fy in range(NY):
        for fc in range(NC):
            for fz in range(NZ):
                pair_z = (fy + fz // 2 + (fz < 2)) % NY
                target = ((fz // 2) * NC + fz % 2) * NZ + 2 * pair_z + fc
                pairs.append(((fy * NC + fc) * NZ + fz, target))
    turned = lax.ppermute(u_half, ("y", "core", "z"), pairs)
    strip = gather(u_half.reshape(3 * half, block), ("y",), NY)
    turned, strip = lax.optimization_barrier((turned, strip))

    inner = [mmt(p_rows[s], turned[t]) for s, t in PAIRS]
    inner_a = jnp.concatenate(inner[:3], axis=0)
    inner_b = jnp.concatenate(inner[3:], axis=0)
    got = send(by_core(core, inner_b, inner_a), "core", 1)
    strip_other = send(strip, "core", 1)
    got, strip_other = lax.optimization_barrier((got, strip_other))
    part = by_core(core, inner_a, inner_b) + got

    strip = strip.reshape(NY, S, 1, half, block)
    strip_other = strip_other.reshape(NY, S, 1, half, block)
    ut = jnp.concatenate(
        [by_core(core, strip, strip_other), by_core(core, strip_other, strip)], axis=2
    ).reshape(NY, S * width, block)

    def turn_z(fy, fc, fz, step):
        return (fz + 2 * fy + fc + 2 * step + (1 if fz == 0 else 0)) % NZ

    def slots_of(z_at, x_at):
        found = number_in((NX * z_at + x_at) * NODE + jnp.arange(NODE, dtype=jnp.int32))
        rank = jnp.cumsum((found >= 0).astype(jnp.int32)) - 1
        ids = jnp.arange(NODE, dtype=jnp.int32)[:, None]
        hit = (found >= 0)[None, :] & (rank[None, :] == ids)
        return jnp.sum(jnp.where(hit, found[None, :], 0), axis=1), rank

    shift = z + group + jnp.where(z == 0, 1, 0)
    near_index = jnp.concatenate(
        [slots_of((shift + 2 * step) % NZ, (x + step) % NX)[0][:2] for step in range(NX)]
    )
    picked = pick(near_index, ut).reshape(NX, 2, NODE, block, block)

    def more(ut):
        index = jnp.concatenate(
            [slots_of((z + group) % NZ, at)[0][2:] for at in range(NX)]
        )
        value = pick(index, ut)
        pairs = []
        for fy in range(NY):
            for fc in range(NC):
                for fz in range(NZ):
                    target = ((fz // 2) * NC + fz % 2) * NZ + (fz + 2 * fy + fc) % NZ
                    pairs.append(((fy * NC + fc) * NZ + fz, target))
        value = lax.ppermute(value, ("y", "core", "z"), pairs)
        value = value.reshape(NX, 2 * NODE, block, block)
        value = lax.all_to_all(value, ("x",), 0, 0, tiled=True)
        return value.reshape(NX, 2, NODE, block, block)

    def none(ut):
        return jnp.zeros((NX, 2, NODE, block, block), BF)

    owners = k_list // NODE
    crowd = jnp.max(jnp.sum((owners[:, None] == owners[None, :]).astype(jnp.int32), axis=1))
    far = lax.cond(crowd > 2, more, none, ut)
    my_slots = slots_of(z, x)[1]

    part, picked = lax.optimization_barrier((part, picked))
    near = []
    for step in range(NX):
        pairs = []
        for fy in range(NY):
            for fc in range(NC):
                for fz in range(NZ):
                    for fx in range(NX):
                        target = ((fz // 2) * NC + fz % 2) * NZ + turn_z(fy, fc, fz, step)
                        pairs.append(
                            (((fy * NC + fc) * NZ + fz) * NX + fx, target * NX + (fx + step) % NX)
                        )
        near.append(lax.ppermute(picked[step], ("y", "core", "z", "x"), pairs))
    pieces = part.reshape(NY * NX, 3 * width // (NY * NX), half)
    part = scatter_sum(pieces, ("y", "x"), y * NX + x)
    sent = part
    for step in (2, 4, 6):
        part = part + send(sent, "z", step)
    part = part.astype(BF)
    other = lax.ppermute(part, "z", [(i, i ^ 1) for i in range(NZ)])
    even = z % 2 == 0
    part = jnp.concatenate(
        [jnp.where(even, part, other), jnp.where(even, other, part)], axis=1
    )
    part, *near = lax.optimization_barrier((part, *near))
    near = jnp.stack(near)
    cross = gather(part, ("y", "x"), NY * NX).reshape(3 * width, width)
    cross_other = send(cross, "core", 1)

    base = patch_strips(ancestor, ut, near, far, row_index, col_index, my_slots, x)
    return patch_corner(base, cross, cross_other, diag_inverse, own_all, row_index, col_index, core)


def solution(mesh):
    fine = Mesh(mesh.devices.reshape(NY, NC, NZ, NX), ("y", "core", "z", "x"))
    row, col = ("y", "core"), ("z", "x")
    in_specs = (P(row, col), P(None, col, row), P(), P(), P())
    return jax.shard_map(
        update_all, mesh=fine, in_specs=in_specs, out_specs=P(row, col), check_vma=False
    )
```

```python
import jax
import jax.numpy as jnp
from jax import lax
from jax.experimental import pallas as pl
from jax.experimental.pallas import tpu as pltpu
from jax.sharding import Mesh, PartitionSpec as P

S = 3
NODE = 4
NY, NC, NZ, NX = 4, 2, 8, 4
SIZES = {"y": NY, "core": NC, "z": NZ, "x": NX}
BF = jnp.bfloat16
F32 = jnp.float32
PAIRS = ((0, 0), (1, 0), (1, 1), (2, 0), (2, 1), (2, 2))
INTERPRET = False


def send(value, axis, step):
    size = SIZES[axis]
    return lax.ppermute(value, axis, [(i, (i + step) % size) for i in range(size)])


def ring_gather(value, axis, begun=None):
    size = SIZES[axis]
    found = [None] * size
    found[0] = value
    ahead = behind = value
    for step in range(1, size // 2):
        if step == 1 and begun is not None:
            behind, ahead = begun
        else:
            behind = send(behind, axis, 1)
            ahead = send(ahead, axis, -1)
        found[step] = ahead
        found[size - step] = behind
    half = value.shape[0] // 2
    found[size // 2] = jnp.concatenate(
        [send(behind[:half], axis, 1), send(ahead[half:], axis, -1)], axis=0
    )
    return found


def place(found, axis, position, dim=0):
    size = SIZES[axis]
    out = None
    for step, part in enumerate(found):
        part = jnp.expand_dims(part, dim)
        if out is None:
            shape = list(part.shape)
            shape[dim] = size
            out = jnp.zeros(shape, part.dtype)
        out = lax.dynamic_update_slice_in_dim(out, part, (position + step) % size, axis=dim)
    return out


def scatter_sum(pieces, axes, position):
    count = pieces.shape[0]
    got = lax.all_to_all(pieces.astype(BF), axes, 0, 0, tiled=True).astype(F32)
    ids = jnp.arange(count, dtype=jnp.int32)[:, None, None]
    return jnp.sum(jnp.where(ids == position, pieces, got), axis=0)


def gather(value, axes, count):
    spread = jnp.broadcast_to(value[None], (count, *value.shape))
    return lax.all_to_all(spread, axes, 0, 0, tiled=True)


def by_core(core, first, second):
    return jnp.where(core == 0, first, second)


def prepare_kernel(flags, at, p_ref, first_ref, second_ref, own_ref):
    wl = p_ref.shape[1]
    block = own_ref.shape[1] // (3 * NODE)
    row_blocks = p_ref.shape[2] // block
    for s in range(S):
        for b in range(row_blocks):
            span = slice(b * block, (b + 1) * block)
            value = p_ref[s, :, span]
            value = jnp.where(flags[s * row_blocks + b] > 0, value, jnp.zeros_like(value))
            if s == 0:
                first_ref[:, span] = value
            else:
                second_ref[(s - 1) * wl : s * wl, span] = value
    for pair, (s, t) in enumerate(((1, 0), (2, 0), (2, 1))):
        for k in range(NODE):
            index = at[t * NODE + k]
            inside = (index >= 0) & (index < row_blocks)
            start = pl.multiple_of(jnp.where(inside, index, 0) * block, block)
            value = p_ref[s, :, pl.ds(start, block)]
            value = jnp.where(inside, value, jnp.zeros_like(value))
            own_ref[:, (pair * NODE + k) * block : (pair * NODE + k + 1) * block] = value


def prepare(panels, listed, at, block):
    _, wl, rows = panels.shape
    return pl.pallas_call(
        prepare_kernel,
        out_shape=(
            jax.ShapeDtypeStruct((wl, rows), BF),
            jax.ShapeDtypeStruct((2 * wl, rows), BF),
            jax.ShapeDtypeStruct((wl, 3 * NODE * block), BF),
        ),
        in_specs=[
            pl.BlockSpec(memory_space=pltpu.SMEM),
            pl.BlockSpec(memory_space=pltpu.SMEM),
            pl.BlockSpec(memory_space=pltpu.VMEM),
        ],
        interpret=INTERPRET,
    )(listed.astype(jnp.int32).reshape(-1), at, panels)


def extract_kernel(pos, *refs):
    first, second = refs[:NZ], refs[NZ : NZ + NX]
    p0, p12, own = refs[NZ + NX :]
    rows = second[0].shape[3]
    block = p0.shape[2]
    lane = pl.multiple_of(pos[2], block)
    for d, ref in enumerate(first):
        at = (pos[0] + d) % NZ
        p0[at] = ref[:, pl.ds(lane, block)]
        own[at] = ref[:, rows:]
    for d, ref in enumerate(second):
        at = (pos[1] + d) % NX
        p12[:, :, pl.ds(at, 1)] = ref[:, :, :, pl.ds(lane, block)][:, :, None]


def extract(first_zx, second_zx, z, x, lane, block, wl):
    second_zx = [part.reshape(2, NZ, wl, -1) for part in second_zx]
    extra = first_zx[0].shape[1] - second_zx[0].shape[3]
    vmem = pl.BlockSpec(memory_space=pltpu.VMEM)
    p0, p12, own = pl.pallas_call(
        extract_kernel,
        out_shape=(
            jax.ShapeDtypeStruct((NZ, NX * wl, block), BF),
            jax.ShapeDtypeStruct((2, NZ, NX, wl, block), BF),
            jax.ShapeDtypeStruct((NZ, NX * wl, extra), BF),
        ),
        in_specs=[pl.BlockSpec(memory_space=pltpu.SMEM), *[vmem] * (NZ + NX)],
        out_specs=(vmem, vmem, vmem),
        interpret=INTERPRET,
    )(jnp.stack([z, x, lane]).astype(jnp.int32), *first_zx, *second_zx)
    width = NZ * NX * wl
    return p0.reshape(width, block), p12.reshape(2, width, block), own.reshape(width, extra)


def pick_kernel(index, pos, ut_ref, out_ref):
    block = ut_ref.shape[2]

    def step(i, carry):
        start = pl.multiple_of(index[i] * block, block)
        for q in range(NODE):
            out_ref[i, q] = ut_ref[(q - pos[1] + NY) % NY, pl.ds(start, block), :]
        return carry

    lax.fori_loop(0, out_ref.shape[0], step, 0)


def pick(index, pos, ut):
    block = ut.shape[2]
    return pl.pallas_call(
        pick_kernel,
        out_shape=jax.ShapeDtypeStruct((index.shape[0], NODE, block, block), BF),
        in_specs=[
            pl.BlockSpec(memory_space=pltpu.SMEM),
            pl.BlockSpec(memory_space=pltpu.SMEM),
            pl.BlockSpec(memory_space=pltpu.VMEM),
        ],
        interpret=INTERPRET,
    )(index, pos, ut)


def strips_kernel(rs, cs, slots, pos, ut, *refs):
    near = refs[:NX]
    far, _, out, buffer, sem_col, sem_row = refs[NX:]
    block = ut.shape[2]
    row_blocks = rs.shape[0]

    def column(j):
        return pltpu.make_async_copy(
            buffer.at[j], out.at[:, pl.ds(j * block, block)], sem_col.at[j]
        )

    for j in range(NODE):
        slot = slots[j]

        @pl.when(cs[j] >= 0)
        def _(j=j, slot=slot):
            for step in range(NX):
                i = (pos[0] - step + NX) % NX

                def fill(q, carry, j=j, slot=slot, step=step, i=i):
                    at = pl.multiple_of((i * NODE + q) * block, block)
                    tile = jnp.where(
                        slot < 2,
                        near[step][jnp.minimum(slot, 1), q],
                        far[i, jnp.maximum(slot - 2, 0), q],
                    )
                    buffer[j, pl.ds(at, block), :] = tile.astype(F32).T.astype(BF)
                    return carry

                lax.fori_loop(0, NODE, fill, 0)
            column(j).start()

    for j in range(NODE):

        @pl.when(cs[j] >= 0)
        def _(j=j):
            column(j).wait()

    def each(act):
        def step(i, carry):
            row = rs[i]

            @pl.when(row >= 0)
            def _():
                for j in range(NODE):
                    act(
                        pltpu.make_async_copy(
                            ut.at[(j - pos[1] + NY) % NY, pl.ds(row * block, block), :],
                            out.at[pl.ds(i * block, block), pl.ds(j * block, block)],
                            sem_row,
                        )
                    )

            return carry

        lax.fori_loop(0, row_blocks, step, 0)

    each(lambda copy: copy.start())
    each(lambda copy: copy.wait())


def patch_strips(ancestor, ut, near, far, row_index, col_index, slots, pos):
    rows, cols = ancestor.shape
    block = cols // NODE
    smem = pl.BlockSpec(memory_space=pltpu.SMEM)
    vmem = pl.BlockSpec(memory_space=pltpu.VMEM)
    anywhere = pl.BlockSpec(memory_space=pl.ANY)
    return pl.pallas_call(
        strips_kernel,
        out_shape=jax.ShapeDtypeStruct((rows, cols), BF),
        in_specs=[smem, smem, smem, smem, *[vmem] * (NX + 2), anywhere],
        out_specs=anywhere,
        scratch_shapes=[
            pltpu.VMEM((NODE, rows, block), BF),
            pltpu.SemaphoreType.DMA((NODE,)),
            pltpu.SemaphoreType.DMA,
        ],
        input_output_aliases={NX + 6: 0},
        interpret=INTERPRET,
    )(row_index, col_index, slots, pos, ut, *near, far, ancestor)


def corner_kernel(
    rs, cs, core, mine, other, diag, own, base, out, cross, kk, sem
):
    width = diag.shape[1]
    block = width // NODE
    for i in range(6):
        rows = slice((i % 3) * width, (i % 3 + 1) * width)
        cross[i] = jnp.where(core[0] == i // 3, mine[rows], other[rows]).astype(F32)
    c = {pair: cross.at[i] for i, pair in enumerate(PAIRS)}
    w10, w20, w21 = (own.at[:, i * width : (i + 1) * width] for i in range(3))

    def at(s, t):
        return kk.at[s * width : (s + 1) * width, t * width : (t + 1) * width]

    def diagonal(s, value):
        return (diag[s] - 0.5 * (value + value.T)).astype(BF)

    def keep(s, t, value):
        at(s, t)[...] = value.astype(BF)
        at(t, s)[...] = value.T.astype(BF)

    at(0, 0)[...] = diagonal(0, c[0, 0][...])
    keep(1, 0, -(c[1, 0][...] + mm(w10[...], at(0, 0)[...])))
    at(1, 1)[...] = diagonal(1, c[1, 1][...] + mm(w10[...], at(0, 1)[...]))
    keep(2, 0, -(c[2, 0][...] + mm(w20[...], at(0, 0)[...]) + mm(w21[...], at(1, 0)[...])))
    keep(2, 1, -(c[2, 1][...] + mm(w20[...], at(0, 1)[...]) + mm(w21[...], at(1, 1)[...])))
    at(2, 2)[...] = diagonal(
        2, c[2, 2][...] + mm(w20[...], at(0, 2)[...]) + mm(w21[...], at(1, 2)[...])
    )

    def each(act):
        def step(i, carry):
            row = rs[i]
            for j in range(NODE):
                col = cs[j]

                @pl.when((row >= 0) & (col >= 0))
                def _():
                    copy = pltpu.make_async_copy(
                        kk.at[pl.ds(row * block, block), pl.ds(col * block, block)],
                        out.at[pl.ds(i * block, block), pl.ds(j * block, block)],
                        sem,
                    )
                    act(copy)

            return carry

        lax.fori_loop(0, rs.shape[0], step, 0)

    each(lambda copy: copy.start())
    each(lambda copy: copy.wait())


def patch_corner(base, mine, other, diag_inverse, own, row_index, col_index, core):
    width = diag_inverse.shape[1]
    smem = pl.BlockSpec(memory_space=pltpu.SMEM)
    vmem = pl.BlockSpec(memory_space=pltpu.VMEM)
    anywhere = pl.BlockSpec(memory_space=pl.ANY)
    return pl.pallas_call(
        corner_kernel,
        out_shape=jax.ShapeDtypeStruct(base.shape, BF),
        in_specs=[smem, smem, smem, vmem, vmem, vmem, vmem, anywhere],
        out_specs=anywhere,
        scratch_shapes=[
            pltpu.VMEM((6, width, width), F32),
            pltpu.VMEM((S * width, S * width), BF),
            pltpu.SemaphoreType.DMA,
        ],
        input_output_aliases={7: 0},
        interpret=INTERPRET,
    )(row_index, col_index, core.astype(jnp.int32).reshape(1), mine, other, diag_inverse, own, base)


def contract(left, right, dims):
    return lax.dot_general(left, right, (dims, ((), ())), preferred_element_type=F32)


def mm(left, right):
    return contract(left, right, ((1,), (0,)))


def mmt(left, right):
    return contract(left, right, ((1,), (1,)))


def update_all(ancestor, panels, diag_inverse, supernode_blocks, row_lists):
    y, core, z, x = (lax.axis_index(name) for name in ("y", "core", "z", "x"))
    rows, cols = ancestor.shape
    block = cols // NODE
    width = NODE * block
    half = width // 2
    wl = panels.shape[1]
    row_blocks = rows // block
    group = 2 * y + core
    first_row = group * row_blocks
    first_col = (NX * z + x) * NODE
    k_list = supernode_blocks.reshape(-1)
    numbers = jnp.arange(S * NODE, dtype=jnp.int32) + 1

    def number_in(ids):
        return jnp.sum(jnp.where(ids[:, None] == k_list[None, :], numbers, 0), axis=1) - 1

    row_ids = first_row + jnp.arange(row_blocks, dtype=jnp.int32)
    row_index = number_in(row_ids)
    col_index = number_in(first_col + jnp.arange(NODE, dtype=jnp.int32))
    listed = jnp.any(row_ids[None, :, None] == row_lists[:, None, :], axis=2)

    def turn_z(fy, fc, fz, step):
        return (fz + 2 * fy + fc + 2 * step + (1 if fz == 0 else 0)) % NZ

    def slots_of(z_at, x_at):
        found = number_in((NX * z_at + x_at) * NODE + jnp.arange(NODE, dtype=jnp.int32))
        rank = jnp.cumsum((found >= 0).astype(jnp.int32)) - 1
        ids = jnp.arange(NODE, dtype=jnp.int32)[:, None]
        hit = (found >= 0)[None, :] & (rank[None, :] == ids)
        return jnp.sum(jnp.where(hit, found[None, :], 0), axis=1), rank

    shift = z + group + jnp.where(z == 0, 1, 0)
    near_index = jnp.concatenate(
        [slots_of((shift + 2 * step) % NZ, (x + step) % NX)[0][:2] for step in range(NX)]
    )
    far_index = jnp.concatenate([slots_of((z + group) % NZ, at)[0][2:] for at in range(NX)])
    owners = k_list // NODE
    crowd = jnp.max(jnp.sum((owners[:, None] == owners[None, :]).astype(jnp.int32), axis=1))
    my_slots = slots_of(z, x)[1]
    pos = jnp.stack([x, y]).astype(jnp.int32)
    my_block = first_col + y
    outside = jnp.all(my_block != k_list)
    keep = jnp.any(my_block == row_lists, axis=1) & outside

    first, second, own = prepare(panels, listed, k_list - first_row, block)

    lane_half = 3 * half
    own_kept = by_core(core, own[:, :lane_half], own[:, lane_half:])
    own_sent = by_core(core, own[:, lane_half:], own[:, :lane_half])
    second_z = gather(second.reshape(2, wl, rows), ("z",), NZ)
    own_kept = own_kept + send(own_sent, "core", 1)
    own_sum = own_kept
    for step in range(1, NY):
        own_sum = own_sum + send(own_kept, "y", step)
    first = jnp.concatenate([first, own_sum], axis=1)
    first_x = [first, send(first, "x", -1), send(first, "x", 2), send(first, "x", 1)]
    first_x = place(first_x, "x", x).reshape(NX * wl, -1)
    indices = (row_index, col_index, near_index, far_index, crowd, my_slots, pos, keep)
    second_z, first_x, indices = lax.optimization_barrier((second_z, first_x, indices))
    row_index, col_index, near_index, far_index, crowd, my_slots, pos, keep = indices
    first_zx = ring_gather(first_x, "z")
    second_z = second_z.transpose(1, 0, 2, 3).reshape(2 * NZ * wl, rows)
    second_zx = ring_gather(second_z, "x")

    active = jnp.where(
        (row_index < 0)[:, None, None], ancestor.reshape(row_blocks, block, cols), 0
    ).reshape(rows, cols)
    q0 = place([mm(part[:, :rows], active) for part in first_zx], "z", z)
    q12 = place(
        [mm(part, active).reshape(2, NZ, wl, cols) for part in second_zx], "x", x, 2
    )
    q0 = q0.reshape(width, cols)
    q12 = q12.reshape(2 * width, cols)

    low = jnp.concatenate([q0, q12[:half]], axis=0)
    high = q12[half:]
    q_chip = by_core(core, low, high) + send(by_core(core, high, low), "core", 1)

    def strip_of(owner):
        return lax.dynamic_slice_in_dim(q_chip, owner * block, block, axis=1)

    q_mine = strip_of(y)
    for step in range(1, NY):
        q_mine = q_mine + send(strip_of((y + step) % NY).astype(BF), "y", step).astype(F32)
    lane = (NX * x + (z // 2 - y - (y == 0)) % NY) * block
    p0, p12, own_mine = extract(first_zx, second_zx, z, x, lane, block, wl)
    p_rows = jnp.concatenate([p0[None], p12], axis=0)
    p_half = jnp.where(z % 2 == 0, p_rows[:, :half], p_rows[:, half:])
    pairs = []
    for fy in range(NY):
        for fc in range(NC):
            for fz in range(NZ):
                pair_z = (fy + fz // 2 + (fz < 2)) % NY
                target = ((fz // 2) * NC + fz % 2) * NZ + 2 * pair_z + fc
                pairs.append((target, (fy * NC + fc) * NZ + fz))
    p_half = lax.ppermute(p_half, ("y", "core", "z"), pairs)
    q_mine, p_half = lax.optimization_barrier((q_mine, p_half))
    q_other = send(q_mine, "core", 1)
    q_low = by_core(core, q_mine, q_other)
    q_high = by_core(core, q_other, q_mine)
    q = (
        q_low[:width],
        jnp.concatenate([q_low[width:], q_high[:half]], axis=0),
        q_high[half:],
    )
    p_other = send(p_half, "core", 1)
    own_other = send(own_mine, "core", 1)
    own_all = jnp.concatenate(
        [by_core(core, own_mine, own_other), by_core(core, own_other, own_mine)], axis=1
    )
    own_all = lax.optimization_barrier(own_all)
    w10, w20, w21 = (own_all[:, i * width : (i + 1) * width] for i in range(3))

    u0 = jnp.where(keep[0], -q[0], 0.0).astype(BF)
    u1 = jnp.where(keep[1], -(q[1] + mm(w10, u0)), 0.0).astype(BF)
    u2 = jnp.where(keep[2], -(q[2] + mm(w20, u0) + mm(w21, u1)), 0.0).astype(BF)
    u = jnp.stack([u0, u1, u2])
    u_half = by_core(core, u[:, :half], u[:, half:])

    p0, p1, p2 = (
        jnp.concatenate(
            [by_core(core, p_half[i], p_other[i]), by_core(core, p_other[i], p_half[i])],
            axis=0,
        )
        for i in range(S)
    )
    left = (by_core(core, p0, p2), by_core(core, p1, p2), by_core(core, p1, p2))
    right = (u0, by_core(core, u0, u1), by_core(core, u1, u2))
    part = jnp.concatenate([mmt(*pair) for pair in zip(left, right)], axis=0)
    strips = []
    for step in range(NY):
        strips.append(send(u_half, "y", NY - step) if step else u_half)
    pieces = part.reshape(NY * NX, 3 * width // (NY * NX), width)
    part = scatter_sum(pieces, ("y", "x"), y * NX + x)
    part, strips = lax.optimization_barrier((part, strips))

    strip = jnp.stack(strips)
    strip_other = send(strip, "core", 1)
    ut = jnp.stack(
        [by_core(core, strip, strip_other), by_core(core, strip_other, strip)], axis=2
    ).reshape(NY, S * width, block)
    picked = pick(near_index, pos, ut).reshape(NX, 2, NODE, block, block)
    part, picked = lax.optimization_barrier((part, picked))
    near = []
    for step in range(NX):
        pairs = []
        for fy in range(NY):
            for fc in range(NC):
                for fz in range(NZ):
                    for fx in range(NX):
                        target = ((fz // 2) * NC + fz % 2) * NZ + turn_z(fy, fc, fz, step)
                        pairs.append(
                            (((fy * NC + fc) * NZ + fz) * NX + fx, target * NX + (fx + step) % NX)
                        )
        near.append(lax.ppermute(picked[step], ("y", "core", "z", "x"), pairs))

    def more(ut):
        value = pick(far_index, pos, ut)
        pairs = []
        for fy in range(NY):
            for fc in range(NC):
                for fz in range(NZ):
                    target = ((fz // 2) * NC + fz % 2) * NZ + (fz + 2 * fy + fc) % NZ
                    pairs.append(((fy * NC + fc) * NZ + fz, target))
        value = lax.ppermute(value, ("y", "core", "z"), pairs)
        value = value.reshape(NX, 2 * NODE, block, block)
        value = lax.all_to_all(value, ("x",), 0, 0, tiled=True)
        return value.reshape(NX, 2, NODE, block, block)

    def none(ut):
        return jnp.zeros((NX, 2, NODE, block, block), BF)

    far = lax.cond(crowd > 2, more, none, ut)

    got = gather(part.astype(BF), ("z",), NZ).astype(F32)
    ids = jnp.arange(NZ, dtype=jnp.int32)[:, None, None]
    part = jnp.sum(jnp.where(ids == z, part[None], got), axis=0).astype(BF)
    cross = gather(part, ("y", "x"), NY * NX).reshape(3 * width, width)
    cross_other = send(cross, "core", 1)

    base = patch_strips(ancestor, ut, near, far, row_index, col_index, my_slots, pos)
    return patch_corner(base, cross, cross_other, diag_inverse, own_all, row_index, col_index, core)


def solution(mesh):
    fine = Mesh(mesh.devices.reshape(NY, NC, NZ, NX), ("y", "core", "z", "x"))
    row, col = ("y", "core"), ("z", "x")
    in_specs = (P(row, col), P(None, col, row), P(), P(), P())
    return jax.shard_map(
        update_all, mesh=fine, in_specs=in_specs, out_specs=P(row, col), check_vma=False
    )
```

```python
import jax
import jax.numpy as jnp
from jax import lax
from jax.experimental import pallas as pl
from jax.experimental.pallas import tpu as pltpu
from jax.sharding import Mesh, PartitionSpec as P

S = 3
NODE = 4
NY, NC, NZ, NX = 4, 2, 8, 4
SIZES = {"y": NY, "core": NC, "z": NZ, "x": NX}
BF = jnp.bfloat16
F32 = jnp.float32
PAIRS = ((0, 0), (1, 0), (1, 1), (2, 0), (2, 1), (2, 2))
INTERPRET = False


def send(value, axis, step):
    size = SIZES[axis]
    return lax.ppermute(value, axis, [(i, (i + step) % size) for i in range(size)])


def ring_gather(value, axis, begun=None):
    size = SIZES[axis]
    found = [None] * size
    found[0] = value
    ahead = behind = value
    for step in range(1, size // 2):
        if step == 1 and begun is not None:
            behind, ahead = begun
        else:
            behind = send(behind, axis, 1)
            ahead = send(ahead, axis, -1)
        found[step] = ahead
        found[size - step] = behind
    half = value.shape[0] // 2
    found[size // 2] = jnp.concatenate(
        [send(behind[:half], axis, 1), send(ahead[half:], axis, -1)], axis=0
    )
    return found


def place(found, axis, position, dim=0):
    size = SIZES[axis]
    out = None
    for step, part in enumerate(found):
        part = jnp.expand_dims(part, dim)
        if out is None:
            shape = list(part.shape)
            shape[dim] = size
            out = jnp.zeros(shape, part.dtype)
        out = lax.dynamic_update_slice_in_dim(out, part, (position + step) % size, axis=dim)
    return out


def scatter_sum(pieces, axes, position):
    count = pieces.shape[0]
    got = lax.all_to_all(pieces.astype(BF), axes, 0, 0, tiled=True).astype(F32)
    ids = jnp.arange(count, dtype=jnp.int32)[:, None, None]
    return jnp.sum(jnp.where(ids == position, pieces, got), axis=0)


def gather(value, axes, count):
    spread = jnp.broadcast_to(value[None], (count, *value.shape))
    return lax.all_to_all(spread, axes, 0, 0, tiled=True)


def by_core(core, first, second):
    return jnp.where(core == 0, first, second)


def prepare_kernel(flags, at, p_ref, first_ref, second_ref, own_ref):
    wl = p_ref.shape[1]
    block = own_ref.shape[1] // (3 * NODE)
    row_blocks = p_ref.shape[2] // block
    for s in range(S):
        for b in range(row_blocks):
            span = slice(b * block, (b + 1) * block)
            value = p_ref[s, :, span]
            value = jnp.where(flags[s * row_blocks + b] > 0, value, jnp.zeros_like(value))
            if s == 0:
                first_ref[:, span] = value
            else:
                second_ref[(s - 1) * wl : s * wl, span] = value
    for pair, (s, t) in enumerate(((1, 0), (2, 0), (2, 1))):
        for k in range(NODE):
            index = at[t * NODE + k]
            inside = (index >= 0) & (index < row_blocks)
            start = pl.multiple_of(jnp.where(inside, index, 0) * block, block)
            value = p_ref[s, :, pl.ds(start, block)]
            value = jnp.where(inside, value, jnp.zeros_like(value))
            own_ref[:, (pair * NODE + k) * block : (pair * NODE + k + 1) * block] = value


def prepare(panels, listed, at, block):
    _, wl, rows = panels.shape
    return pl.pallas_call(
        prepare_kernel,
        out_shape=(
            jax.ShapeDtypeStruct((wl, rows), BF),
            jax.ShapeDtypeStruct((2 * wl, rows), BF),
            jax.ShapeDtypeStruct((wl, 3 * NODE * block), BF),
        ),
        in_specs=[
            pl.BlockSpec(memory_space=pltpu.SMEM),
            pl.BlockSpec(memory_space=pltpu.SMEM),
            pl.BlockSpec(memory_space=pltpu.VMEM),
        ],
        interpret=INTERPRET,
    )(listed.astype(jnp.int32).reshape(-1), at, panels)


def extract_kernel(pos, *refs):
    first, second = refs[:NZ], refs[NZ : NZ + NX]
    p0, p12, own = refs[NZ + NX :]
    rows = second[0].shape[3]
    block = p0.shape[2]
    lane = pl.multiple_of(pos[2], block)
    for d, ref in enumerate(first):
        at = (pos[0] + d) % NZ
        p0[at] = ref[:, pl.ds(lane, block)]
        own[at] = ref[:, rows:]
    for d, ref in enumerate(second):
        at = (pos[1] + d) % NX
        p12[:, :, pl.ds(at, 1)] = ref[:, :, :, pl.ds(lane, block)][:, :, None]


def extract(first_zx, second_zx, z, x, lane, block, wl):
    second_zx = [part.reshape(2, NZ, wl, -1) for part in second_zx]
    extra = first_zx[0].shape[1] - second_zx[0].shape[3]
    vmem = pl.BlockSpec(memory_space=pltpu.VMEM)
    p0, p12, own = pl.pallas_call(
        extract_kernel,
        out_shape=(
            jax.ShapeDtypeStruct((NZ, NX * wl, block), BF),
            jax.ShapeDtypeStruct((2, NZ, NX, wl, block), BF),
            jax.ShapeDtypeStruct((NZ, NX * wl, extra), BF),
        ),
        in_specs=[pl.BlockSpec(memory_space=pltpu.SMEM), *[vmem] * (NZ + NX)],
        out_specs=(vmem, vmem, vmem),
        interpret=INTERPRET,
    )(jnp.stack([z, x, lane]).astype(jnp.int32), *first_zx, *second_zx)
    width = NZ * NX * wl
    return p0.reshape(width, block), p12.reshape(2, width, block), own.reshape(width, extra)


def pick_kernel(index, pos, ut_ref, out_ref):
    block = ut_ref.shape[2]

    def step(i, carry):
        start = pl.multiple_of(index[i] * block, block)
        for q in range(NODE):
            out_ref[i, q] = ut_ref[(q - pos[1] + NY) % NY, pl.ds(start, block), :]
        return carry

    lax.fori_loop(0, out_ref.shape[0], step, 0)


def pick(index, pos, ut):
    block = ut.shape[2]
    return pl.pallas_call(
        pick_kernel,
        out_shape=jax.ShapeDtypeStruct((index.shape[0], NODE, block, block), BF),
        in_specs=[
            pl.BlockSpec(memory_space=pltpu.SMEM),
            pl.BlockSpec(memory_space=pltpu.SMEM),
            pl.BlockSpec(memory_space=pltpu.VMEM),
        ],
        interpret=INTERPRET,
    )(index, pos, ut)


def strips_kernel(rs, cs, slots, pos, ut, *refs):
    near = refs[:NX]
    far, _, out, buffer, sem_col, sem_row = refs[NX:]
    block = ut.shape[2]
    row_blocks = rs.shape[0]

    def column(j):
        return pltpu.make_async_copy(
            buffer.at[j], out.at[:, pl.ds(j * block, block)], sem_col.at[j]
        )

    for j in range(NODE):
        slot = slots[j]

        @pl.when(cs[j] >= 0)
        def _(j=j, slot=slot):
            for step in range(NX):
                i = (pos[0] - step + NX) % NX

                def fill(q, carry, j=j, slot=slot, step=step, i=i):
                    at = pl.multiple_of((i * NODE + q) * block, block)
                    tile = jnp.where(
                        slot < 2,
                        near[step][jnp.minimum(slot, 1), q],
                        far[i, jnp.maximum(slot - 2, 0), q],
                    )
                    buffer[j, pl.ds(at, block), :] = tile.astype(F32).T.astype(BF)
                    return carry

                lax.fori_loop(0, NODE, fill, 0)
            column(j).start()

    for j in range(NODE):

        @pl.when(cs[j] >= 0)
        def _(j=j):
            column(j).wait()

    def each(act):
        def step(i, carry):
            row = rs[i]

            @pl.when(row >= 0)
            def _():
                for j in range(NODE):
                    act(
                        pltpu.make_async_copy(
                            ut.at[(j - pos[1] + NY) % NY, pl.ds(row * block, block), :],
                            out.at[pl.ds(i * block, block), pl.ds(j * block, block)],
                            sem_row,
                        )
                    )

            return carry

        lax.fori_loop(0, row_blocks, step, 0)

    each(lambda copy: copy.start())
    each(lambda copy: copy.wait())


def patch_strips(ancestor, ut, near, far, row_index, col_index, slots, pos):
    rows, cols = ancestor.shape
    block = cols // NODE
    smem = pl.BlockSpec(memory_space=pltpu.SMEM)
    vmem = pl.BlockSpec(memory_space=pltpu.VMEM)
    anywhere = pl.BlockSpec(memory_space=pl.ANY)
    return pl.pallas_call(
        strips_kernel,
        out_shape=jax.ShapeDtypeStruct((rows, cols), BF),
        in_specs=[smem, smem, smem, smem, *[vmem] * (NX + 2), anywhere],
        out_specs=anywhere,
        scratch_shapes=[
            pltpu.VMEM((NODE, rows, block), BF),
            pltpu.SemaphoreType.DMA((NODE,)),
            pltpu.SemaphoreType.DMA,
        ],
        input_output_aliases={NX + 6: 0},
        interpret=INTERPRET,
    )(row_index, col_index, slots, pos, ut, *near, far, ancestor)


def corner_kernel(
    rs, cs, core, mine, other, diag, own, base, out, cross, kk, sem
):
    width = diag.shape[1]
    block = width // NODE
    for i in range(6):
        rows = slice((i % 3) * width, (i % 3 + 1) * width)
        cross[i] = jnp.where(core[0] == i // 3, mine[rows], other[rows]).astype(F32)
    c = {pair: cross.at[i] for i, pair in enumerate(PAIRS)}
    w10, w20, w21 = (own.at[:, i * width : (i + 1) * width] for i in range(3))

    def at(s, t):
        return kk.at[s * width : (s + 1) * width, t * width : (t + 1) * width]

    def diagonal(s, value):
        return (diag[s] - 0.5 * (value + value.T)).astype(BF)

    def keep(s, t, value):
        at(s, t)[...] = value.astype(BF)
        at(t, s)[...] = value.T.astype(BF)

    at(0, 0)[...] = diagonal(0, c[0, 0][...])
    keep(1, 0, -(c[1, 0][...] + mm(w10[...], at(0, 0)[...])))
    at(1, 1)[...] = diagonal(1, c[1, 1][...] + mm(w10[...], at(0, 1)[...]))
    keep(2, 0, -(c[2, 0][...] + mm(w20[...], at(0, 0)[...]) + mm(w21[...], at(1, 0)[...])))
    keep(2, 1, -(c[2, 1][...] + mm(w20[...], at(0, 1)[...]) + mm(w21[...], at(1, 1)[...])))
    at(2, 2)[...] = diagonal(
        2, c[2, 2][...] + mm(w20[...], at(0, 2)[...]) + mm(w21[...], at(1, 2)[...])
    )

    def each(act):
        def step(i, carry):
            row = rs[i]
            for j in range(NODE):
                col = cs[j]

                @pl.when((row >= 0) & (col >= 0))
                def _():
                    copy = pltpu.make_async_copy(
                        kk.at[pl.ds(row * block, block), pl.ds(col * block, block)],
                        out.at[pl.ds(i * block, block), pl.ds(j * block, block)],
                        sem,
                    )
                    act(copy)

            return carry

        lax.fori_loop(0, rs.shape[0], step, 0)

    each(lambda copy: copy.start())
    each(lambda copy: copy.wait())


def patch_corner(base, mine, other, diag_inverse, own, row_index, col_index, core):
    width = diag_inverse.shape[1]
    smem = pl.BlockSpec(memory_space=pltpu.SMEM)
    vmem = pl.BlockSpec(memory_space=pltpu.VMEM)
    anywhere = pl.BlockSpec(memory_space=pl.ANY)
    return pl.pallas_call(
        corner_kernel,
        out_shape=jax.ShapeDtypeStruct(base.shape, BF),
        in_specs=[smem, smem, smem, vmem, vmem, vmem, vmem, anywhere],
        out_specs=anywhere,
        scratch_shapes=[
            pltpu.VMEM((6, width, width), F32),
            pltpu.VMEM((S * width, S * width), BF),
            pltpu.SemaphoreType.DMA,
        ],
        input_output_aliases={7: 0},
        interpret=INTERPRET,
    )(row_index, col_index, core.astype(jnp.int32).reshape(1), mine, other, diag_inverse, own, base)


def contract(left, right, dims):
    return lax.dot_general(left, right, (dims, ((), ())), preferred_element_type=F32)


def mm(left, right):
    return contract(left, right, ((1,), (0,)))


def mmt(left, right):
    return contract(left, right, ((1,), (1,)))


def update_all(ancestor, panels, diag_inverse, supernode_blocks, row_lists):
    y, core, z, x = (lax.axis_index(name) for name in ("y", "core", "z", "x"))
    rows, cols = ancestor.shape
    block = cols // NODE
    width = NODE * block
    half = width // 2
    wl = panels.shape[1]
    row_blocks = rows // block
    group = 2 * y + core
    first_row = group * row_blocks
    first_col = (NX * z + x) * NODE
    k_list = supernode_blocks.reshape(-1)
    numbers = jnp.arange(S * NODE, dtype=jnp.int32) + 1

    def number_in(ids):
        return jnp.sum(jnp.where(ids[:, None] == k_list[None, :], numbers, 0), axis=1) - 1

    row_ids = first_row + jnp.arange(row_blocks, dtype=jnp.int32)
    row_index = number_in(row_ids)
    col_index = number_in(first_col + jnp.arange(NODE, dtype=jnp.int32))
    listed = jnp.any(row_ids[None, :, None] == row_lists[:, None, :], axis=2)

    def turn_z(fy, fc, fz, step):
        return (fz + 2 * fy + fc + 2 * step + (1 if fz == 0 else 0)) % NZ

    def slots_of(z_at, x_at):
        found = number_in((NX * z_at + x_at) * NODE + jnp.arange(NODE, dtype=jnp.int32))
        rank = jnp.cumsum((found >= 0).astype(jnp.int32)) - 1
        ids = jnp.arange(NODE, dtype=jnp.int32)[:, None]
        hit = (found >= 0)[None, :] & (rank[None, :] == ids)
        return jnp.sum(jnp.where(hit, found[None, :], 0), axis=1), rank

    shift = z + group + jnp.where(z == 0, 1, 0)
    near_index = jnp.concatenate(
        [slots_of((shift + 2 * step) % NZ, (x + step) % NX)[0][:2] for step in range(NX)]
    )
    far_index = jnp.concatenate([slots_of((z + group) % NZ, at)[0][2:] for at in range(NX)])
    owners = k_list // NODE
    crowd = jnp.max(jnp.sum((owners[:, None] == owners[None, :]).astype(jnp.int32), axis=1))
    my_slots = slots_of(z, x)[1]
    pos = jnp.stack([x, y]).astype(jnp.int32)
    my_block = first_col + y
    outside = jnp.all(my_block != k_list)
    keep = jnp.any(my_block == row_lists, axis=1) & outside

    first, second, own = prepare(panels, listed, k_list - first_row, block)

    lane_half = 3 * half
    own_kept = by_core(core, own[:, :lane_half], own[:, lane_half:])
    own_sent = by_core(core, own[:, lane_half:], own[:, :lane_half])
    second_z = gather(second.reshape(2, wl, rows), ("z",), NZ)
    own_kept = own_kept + send(own_sent, "core", 1)
    own_sum = own_kept
    for step in range(1, NY):
        own_sum = own_sum + send(own_kept, "y", step)
    first = jnp.concatenate([first, own_sum], axis=1)
    first_x = [first, send(first, "x", -1), send(first, "x", 2), send(first, "x", 1)]
    first_x = place(first_x, "x", x).reshape(NX * wl, -1)
    indices = (row_index, col_index, near_index, far_index, crowd, my_slots, pos, keep)
    second_z, first_x, indices = lax.optimization_barrier((second_z, first_x, indices))
    row_index, col_index, near_index, far_index, crowd, my_slots, pos, keep = indices
    first_zx = ring_gather(first_x, "z")
    second_z = second_z.transpose(1, 0, 2, 3).reshape(2 * NZ * wl, rows)
    second_zx = ring_gather(second_z, "x")

    active = jnp.where(
        (row_index < 0)[:, None, None], ancestor.reshape(row_blocks, block, cols), 0
    ).reshape(rows, cols)
    q0 = place([mm(part[:, :rows], active) for part in first_zx], "z", z)
    q12 = place(
        [mm(part, active).reshape(2, NZ, wl, cols) for part in second_zx], "x", x, 2
    )
    q0 = q0.reshape(width, cols)
    q12 = q12.reshape(2 * width, cols)

    low = jnp.concatenate([q0, q12[:half]], axis=0)
    high = q12[half:]
    q_chip = by_core(core, low, high) + send(by_core(core, high, low), "core", 1)

    def strip_of(owner):
        return lax.dynamic_slice_in_dim(q_chip, owner * block, block, axis=1)

    q_mine = strip_of(y)
    for step in range(1, NY):
        got = send(strip_of((y + step) % NY).astype(BF), "y", step)
        q_mine = q_mine + got.astype(F32)
    lane = (NX * x + (z // 2 - y - (y == 0)) % NY) * block
    p0, p12, own_mine = extract(first_zx, second_zx, z, x, lane, block, wl)
    p_rows = jnp.concatenate([p0[None], p12], axis=0)
    p_half = jnp.where(z % 2 == 0, p_rows[:, :half], p_rows[:, half:])
    pairs = []
    for fy in range(NY):
        for fc in range(NC):
            for fz in range(NZ):
                pair_z = (fy + fz // 2 + (fz < 2)) % NY
                target = ((fz // 2) * NC + fz % 2) * NZ + 2 * pair_z + fc
                pairs.append((target, (fy * NC + fc) * NZ + fz))
    p_half = lax.ppermute(p_half, ("y", "core", "z"), pairs)
    q_mine, p_half = lax.optimization_barrier((q_mine, p_half))
    q_other = send(q_mine, "core", 1)
    q_low = by_core(core, q_mine, q_other)
    q_high = by_core(core, q_other, q_mine)
    q = (
        q_low[:width],
        jnp.concatenate([q_low[width:], q_high[:half]], axis=0),
        q_high[half:],
    )
    p_other = send(p_half, "core", 1)
    own_other = send(own_mine, "core", 1)
    own_all = jnp.concatenate(
        [by_core(core, own_mine, own_other), by_core(core, own_other, own_mine)], axis=1
    )
    own_all = lax.optimization_barrier(own_all)
    w10, w20, w21 = (own_all[:, i * width : (i + 1) * width] for i in range(3))

    u0 = jnp.where(keep[0], -q[0], 0.0).astype(BF)
    u1 = jnp.where(keep[1], -(q[1] + mm(w10, u0)), 0.0).astype(BF)
    u2 = jnp.where(keep[2], -(q[2] + mm(w20, u0) + mm(w21, u1)), 0.0).astype(BF)
    u = jnp.stack([u0, u1, u2])
    u_half = by_core(core, u[:, :half], u[:, half:])

    p0, p1, p2 = (
        jnp.concatenate(
            [by_core(core, p_half[i], p_other[i]), by_core(core, p_other[i], p_half[i])],
            axis=0,
        )
        for i in range(S)
    )
    left = (by_core(core, p0, p2), by_core(core, p1, p2), by_core(core, p1, p2))
    right = (u0, by_core(core, u0, u1), by_core(core, u1, u2))
    part = jnp.concatenate([mmt(*pair) for pair in zip(left, right)], axis=0)
    strips = []
    for step in range(NY):
        strips.append(send(u_half, "y", NY - step) if step else u_half)
    pieces = part.reshape(NY * NX, 3 * width // (NY * NX), width)
    part = scatter_sum(pieces, ("y", "x"), y * NX + x)

    strip = jnp.stack(strips)
    strip_other = send(strip, "core", 1)
    ut = jnp.stack(
        [by_core(core, strip, strip_other), by_core(core, strip_other, strip)], axis=2
    ).reshape(NY, S * width, block)
    picked = pick(near_index, pos, ut).reshape(NX, 2, NODE, block, block)
    near = []
    for step in range(NX):
        pairs = []
        for fy in range(NY):
            for fc in range(NC):
                for fz in range(NZ):
                    for fx in range(NX):
                        target = ((fz // 2) * NC + fz % 2) * NZ + turn_z(fy, fc, fz, step)
                        pairs.append(
                            (((fy * NC + fc) * NZ + fz) * NX + fx, target * NX + (fx + step) % NX)
                        )
        near.append(lax.ppermute(picked[step], ("y", "core", "z", "x"), pairs))

    def more(ut):
        value = pick(far_index, pos, ut)
        pairs = []
        for fy in range(NY):
            for fc in range(NC):
                for fz in range(NZ):
                    target = ((fz // 2) * NC + fz % 2) * NZ + (fz + 2 * fy + fc) % NZ
                    pairs.append(((fy * NC + fc) * NZ + fz, target))
        value = lax.ppermute(value, ("y", "core", "z"), pairs)
        value = value.reshape(NX, 2 * NODE, block, block)
        value = lax.all_to_all(value, ("x",), 0, 0, tiled=True)
        return value.reshape(NX, 2, NODE, block, block)

    def none(ut):
        return jnp.zeros((NX, 2, NODE, block, block), BF)

    part, ut_late = lax.optimization_barrier((part, ut))
    far = lax.cond(crowd > 2, more, none, ut_late)
    part, far = lax.optimization_barrier((part, far))

    got = gather(part.astype(BF), ("z",), NZ)
    ids = jnp.arange(NZ, dtype=jnp.int32)[:, None, None]
    got = jnp.where(ids == z, part[None], got.astype(F32))
    part = jnp.sum(got, axis=0).astype(BF)
    cross = gather(part, ("y", "x"), NY * NX).reshape(3 * width, width)
    cross_other = send(cross, "core", 1)

    base = patch_strips(
        ancestor, ut, near, far, row_index, col_index, my_slots, pos
    )
    return patch_corner(base, cross, cross_other, diag_inverse, own_all, row_index, col_index, core)


def solution(mesh):
    fine = Mesh(mesh.devices.reshape(NY, NC, NZ, NX), ("y", "core", "z", "x"))
    row, col = ("y", "core"), ("z", "x")
    in_specs = (P(row, col), P(None, col, row), P(), P(), P())
    return jax.shard_map(
        update_all, mesh=fine, in_specs=in_specs, out_specs=P(row, col), check_vma=False
    )
```

```python
import jax
import jax.numpy as jnp
from jax import lax
from jax.experimental import pallas as pl
from jax.experimental.pallas import tpu as pltpu
from jax.sharding import Mesh, PartitionSpec as P

S = 3
NODE = 4
NY, NC, NZ, NX = 4, 2, 8, 4
SIZES = {"y": NY, "core": NC, "z": NZ, "x": NX}
BF = jnp.bfloat16
F32 = jnp.float32
PAIRS = ((0, 0), (1, 0), (1, 1), (2, 0), (2, 1), (2, 2))
INTERPRET = False


def send(value, axis, step):
    size = SIZES[axis]
    return lax.ppermute(value, axis, [(i, (i + step) % size) for i in range(size)])


def ring_gather(value, axis, begun=None):
    size = SIZES[axis]
    found = [None] * size
    found[0] = value
    ahead = behind = value
    for step in range(1, size // 2):
        if step == 1 and begun is not None:
            behind, ahead = begun
        else:
            behind = send(behind, axis, 1)
            ahead = send(ahead, axis, -1)
        found[step] = ahead
        found[size - step] = behind
    half = value.shape[0] // 2
    found[size // 2] = jnp.concatenate(
        [send(behind[:half], axis, 1), send(ahead[half:], axis, -1)], axis=0
    )
    return found


def place(found, axis, position, dim=0):
    size = SIZES[axis]
    out = None
    for step, part in enumerate(found):
        part = jnp.expand_dims(part, dim)
        if out is None:
            shape = list(part.shape)
            shape[dim] = size
            out = jnp.zeros(shape, part.dtype)
        out = lax.dynamic_update_slice_in_dim(out, part, (position + step) % size, axis=dim)
    return out


def scatter_sum(pieces, axes, position):
    count = pieces.shape[0]
    got = lax.all_to_all(pieces.astype(BF), axes, 0, 0, tiled=True).astype(F32)
    ids = jnp.arange(count, dtype=jnp.int32)[:, None, None]
    return jnp.sum(jnp.where(ids == position, pieces, got), axis=0)


def gather(value, axes, count):
    spread = jnp.broadcast_to(value[None], (count, *value.shape))
    return lax.all_to_all(spread, axes, 0, 0, tiled=True)


def by_core(core, first, second):
    return jnp.where(core == 0, first, second)


def prepare_kernel(flags, at, p_ref, first_ref, second_ref, own_ref):
    wl = p_ref.shape[1]
    block = own_ref.shape[1] // (3 * NODE)
    row_blocks = p_ref.shape[2] // block
    for s in range(S):
        for b in range(row_blocks):
            span = slice(b * block, (b + 1) * block)
            value = p_ref[s, :, span]
            value = jnp.where(flags[s * row_blocks + b] > 0, value, jnp.zeros_like(value))
            if s == 0:
                first_ref[:, span] = value
            else:
                second_ref[(s - 1) * wl : s * wl, span] = value
    for pair, (s, t) in enumerate(((1, 0), (2, 0), (2, 1))):
        for k in range(NODE):
            index = at[t * NODE + k]
            inside = (index >= 0) & (index < row_blocks)
            start = pl.multiple_of(jnp.where(inside, index, 0) * block, block)
            value = p_ref[s, :, pl.ds(start, block)]
            value = jnp.where(inside, value, jnp.zeros_like(value))
            own_ref[:, (pair * NODE + k) * block : (pair * NODE + k + 1) * block] = value


def prepare(panels, listed, at, block):
    _, wl, rows = panels.shape
    return pl.pallas_call(
        prepare_kernel,
        out_shape=(
            jax.ShapeDtypeStruct((wl, rows), BF),
            jax.ShapeDtypeStruct((2 * wl, rows), BF),
            jax.ShapeDtypeStruct((wl, 3 * NODE * block), BF),
        ),
        in_specs=[
            pl.BlockSpec(memory_space=pltpu.SMEM),
            pl.BlockSpec(memory_space=pltpu.SMEM),
            pl.BlockSpec(memory_space=pltpu.VMEM),
        ],
        interpret=INTERPRET,
    )(listed.astype(jnp.int32).reshape(-1), at, panels)


def extract_kernel(pos, *refs):
    first, second = refs[:NZ], refs[NZ : NZ + NX]
    p0, p12, own = refs[NZ + NX :]
    rows = second[0].shape[3]
    block = p0.shape[2]
    lane = pl.multiple_of(pos[2], block)
    for d, ref in enumerate(first):
        at = (pos[0] + d) % NZ
        p0[at] = ref[:, pl.ds(lane, block)]
        own[at] = ref[:, rows:]
    for d, ref in enumerate(second):
        at = (pos[1] + d) % NX
        p12[:, :, pl.ds(at, 1)] = ref[:, :, :, pl.ds(lane, block)][:, :, None]


def extract(first_zx, second_zx, z, x, lane, block, wl):
    second_zx = [part.reshape(2, NZ, wl, -1) for part in second_zx]
    extra = first_zx[0].shape[1] - second_zx[0].shape[3]
    vmem = pl.BlockSpec(memory_space=pltpu.VMEM)
    p0, p12, own = pl.pallas_call(
        extract_kernel,
        out_shape=(
            jax.ShapeDtypeStruct((NZ, NX * wl, block), BF),
            jax.ShapeDtypeStruct((2, NZ, NX, wl, block), BF),
            jax.ShapeDtypeStruct((NZ, NX * wl, extra), BF),
        ),
        in_specs=[pl.BlockSpec(memory_space=pltpu.SMEM), *[vmem] * (NZ + NX)],
        out_specs=(vmem, vmem, vmem),
        interpret=INTERPRET,
    )(jnp.stack([z, x, lane]).astype(jnp.int32), *first_zx, *second_zx)
    width = NZ * NX * wl
    return p0.reshape(width, block), p12.reshape(2, width, block), own.reshape(width, extra)


def pick_kernel(index, pos, ut_ref, out_ref):
    block = ut_ref.shape[2]

    def step(i, carry):
        start = pl.multiple_of(index[i] * block, block)
        for q in range(NODE):
            out_ref[i, q] = ut_ref[(q - pos[1] + NY) % NY, pl.ds(start, block), :]
        return carry

    lax.fori_loop(0, out_ref.shape[0], step, 0)


def pick(index, pos, ut):
    block = ut.shape[2]
    return pl.pallas_call(
        pick_kernel,
        out_shape=jax.ShapeDtypeStruct((index.shape[0], NODE, block, block), BF),
        in_specs=[
            pl.BlockSpec(memory_space=pltpu.SMEM),
            pl.BlockSpec(memory_space=pltpu.SMEM),
            pl.BlockSpec(memory_space=pltpu.VMEM),
        ],
        interpret=INTERPRET,
    )(index, pos, ut)


def strips_kernel(rs, cs, slots, pos, ut, *refs):
    near = refs[:NX]
    far, _, out, buffer, sem_col, sem_row = refs[NX:]
    block = ut.shape[2]
    row_blocks = rs.shape[0]

    def column(j):
        return pltpu.make_async_copy(
            buffer.at[j], out.at[:, pl.ds(j * block, block)], sem_col.at[j]
        )

    for j in range(NODE):
        slot = slots[j]

        @pl.when(cs[j] >= 0)
        def _(j=j, slot=slot):
            for step in range(NX):
                i = (pos[0] - step + NX) % NX

                def fill(q, carry, j=j, slot=slot, step=step, i=i):
                    at = pl.multiple_of((i * NODE + q) * block, block)
                    tile = jnp.where(
                        slot < 2,
                        near[step][jnp.minimum(slot, 1), q],
                        far[i, jnp.maximum(slot - 2, 0), q],
                    )
                    buffer[j, pl.ds(at, block), :] = tile.astype(F32).T.astype(BF)
                    return carry

                lax.fori_loop(0, NODE, fill, 0)
            column(j).start()

    for j in range(NODE):

        @pl.when(cs[j] >= 0)
        def _(j=j):
            column(j).wait()

    def each(act):
        def step(i, carry):
            row = rs[i]

            @pl.when(row >= 0)
            def _():
                for j in range(NODE):
                    act(
                        pltpu.make_async_copy(
                            ut.at[(j - pos[1] + NY) % NY, pl.ds(row * block, block), :],
                            out.at[pl.ds(i * block, block), pl.ds(j * block, block)],
                            sem_row,
                        )
                    )

            return carry

        lax.fori_loop(0, row_blocks, step, 0)

    each(lambda copy: copy.start())
    each(lambda copy: copy.wait())


def patch_strips(ancestor, ut, near, far, row_index, col_index, slots, pos):
    rows, cols = ancestor.shape
    block = cols // NODE
    smem = pl.BlockSpec(memory_space=pltpu.SMEM)
    vmem = pl.BlockSpec(memory_space=pltpu.VMEM)
    anywhere = pl.BlockSpec(memory_space=pl.ANY)
    return pl.pallas_call(
        strips_kernel,
        out_shape=jax.ShapeDtypeStruct((rows, cols), BF),
        in_specs=[smem, smem, smem, smem, *[vmem] * (NX + 2), anywhere],
        out_specs=anywhere,
        scratch_shapes=[
            pltpu.VMEM((NODE, rows, block), BF),
            pltpu.SemaphoreType.DMA((NODE,)),
            pltpu.SemaphoreType.DMA,
        ],
        input_output_aliases={NX + 6: 0},
        interpret=INTERPRET,
    )(row_index, col_index, slots, pos, ut, *near, far, ancestor)


def corner_kernel(
    rs, cs, core, mine, other, diag, own, base, out, cross, kk, sem
):
    width = diag.shape[1]
    block = width // NODE
    for i in range(6):
        rows = slice((i % 3) * width, (i % 3 + 1) * width)
        cross[i] = jnp.where(core[0] == i // 3, mine[rows], other[rows]).astype(F32)
    c = {pair: cross.at[i] for i, pair in enumerate(PAIRS)}
    w10, w20, w21 = (own.at[:, i * width : (i + 1) * width] for i in range(3))

    def at(s, t):
        return kk.at[s * width : (s + 1) * width, t * width : (t + 1) * width]

    def diagonal(s, value):
        return (diag[s] - 0.5 * (value + value.T)).astype(BF)

    def keep(s, t, value):
        at(s, t)[...] = value.astype(BF)
        at(t, s)[...] = value.T.astype(BF)

    at(0, 0)[...] = diagonal(0, c[0, 0][...])
    keep(1, 0, -(c[1, 0][...] + mm(w10[...], at(0, 0)[...])))
    at(1, 1)[...] = diagonal(1, c[1, 1][...] + mm(w10[...], at(0, 1)[...]))
    keep(2, 0, -(c[2, 0][...] + mm(w20[...], at(0, 0)[...]) + mm(w21[...], at(1, 0)[...])))
    keep(2, 1, -(c[2, 1][...] + mm(w20[...], at(0, 1)[...]) + mm(w21[...], at(1, 1)[...])))
    at(2, 2)[...] = diagonal(
        2, c[2, 2][...] + mm(w20[...], at(0, 2)[...]) + mm(w21[...], at(1, 2)[...])
    )

    def each(act):
        def step(i, carry):
            row = rs[i]
            for j in range(NODE):
                col = cs[j]

                @pl.when((row >= 0) & (col >= 0))
                def _():
                    copy = pltpu.make_async_copy(
                        kk.at[pl.ds(row * block, block), pl.ds(col * block, block)],
                        out.at[pl.ds(i * block, block), pl.ds(j * block, block)],
                        sem,
                    )
                    act(copy)

            return carry

        lax.fori_loop(0, rs.shape[0], step, 0)

    each(lambda copy: copy.start())
    each(lambda copy: copy.wait())


def patch_corner(base, mine, other, diag_inverse, own, row_index, col_index, core):
    width = diag_inverse.shape[1]
    smem = pl.BlockSpec(memory_space=pltpu.SMEM)
    vmem = pl.BlockSpec(memory_space=pltpu.VMEM)
    anywhere = pl.BlockSpec(memory_space=pl.ANY)
    return pl.pallas_call(
        corner_kernel,
        out_shape=jax.ShapeDtypeStruct(base.shape, BF),
        in_specs=[smem, smem, smem, vmem, vmem, vmem, vmem, anywhere],
        out_specs=anywhere,
        scratch_shapes=[
            pltpu.VMEM((6, width, width), F32),
            pltpu.VMEM((S * width, S * width), BF),
            pltpu.SemaphoreType.DMA,
        ],
        input_output_aliases={7: 0},
        interpret=INTERPRET,
    )(row_index, col_index, core.astype(jnp.int32).reshape(1), mine, other, diag_inverse, own, base)


def contract(left, right, dims):
    return lax.dot_general(left, right, (dims, ((), ())), preferred_element_type=F32)


def mm(left, right):
    return contract(left, right, ((1,), (0,)))


def mmt(left, right):
    return contract(left, right, ((1,), (1,)))


def update_all(ancestor, panels, diag_inverse, supernode_blocks, row_lists):
    y, core, z, x = (lax.axis_index(name) for name in ("y", "core", "z", "x"))
    rows, cols = ancestor.shape
    block = cols // NODE
    width = NODE * block
    half = width // 2
    wl = panels.shape[1]
    row_blocks = rows // block
    group = 2 * y + core
    first_row = group * row_blocks
    first_col = (NX * z + x) * NODE
    k_list = supernode_blocks.reshape(-1)
    numbers = jnp.arange(S * NODE, dtype=jnp.int32) + 1

    def number_in(ids):
        return jnp.sum(jnp.where(ids[:, None] == k_list[None, :], numbers, 0), axis=1) - 1

    row_ids = first_row + jnp.arange(row_blocks, dtype=jnp.int32)
    row_index = number_in(row_ids)
    col_index = number_in(first_col + jnp.arange(NODE, dtype=jnp.int32))
    listed = jnp.any(row_ids[None, :, None] == row_lists[:, None, :], axis=2)

    def turn_z(fy, fc, fz, step):
        return (fz + 2 * fy + fc + 2 * step + (1 if fz == 0 else 0)) % NZ

    def slots_of(z_at, x_at):
        found = number_in((NX * z_at + x_at) * NODE + jnp.arange(NODE, dtype=jnp.int32))
        rank = jnp.cumsum((found >= 0).astype(jnp.int32)) - 1
        ids = jnp.arange(NODE, dtype=jnp.int32)[:, None]
        hit = (found >= 0)[None, :] & (rank[None, :] == ids)
        return jnp.sum(jnp.where(hit, found[None, :], 0), axis=1), rank

    shift = z + group + jnp.where(z == 0, 1, 0)
    near_index = jnp.concatenate(
        [slots_of((shift + 2 * step) % NZ, (x + step) % NX)[0][:2] for step in range(NX)]
    )
    far_index = jnp.concatenate([slots_of((z + group) % NZ, at)[0][2:] for at in range(NX)])
    owners = k_list // NODE
    crowd = jnp.max(jnp.sum((owners[:, None] == owners[None, :]).astype(jnp.int32), axis=1))
    my_slots = slots_of(z, x)[1]
    pos = jnp.stack([x, y]).astype(jnp.int32)
    my_block = first_col + y
    outside = jnp.all(my_block != k_list)
    keep = jnp.any(my_block == row_lists, axis=1) & outside

    first, second, own = prepare(panels, listed, k_list - first_row, block)

    lane_half = 3 * half
    own_kept = by_core(core, own[:, :lane_half], own[:, lane_half:])
    own_sent = by_core(core, own[:, lane_half:], own[:, :lane_half])
    second_z = gather(second.reshape(2, wl, rows), ("z",), NZ)
    own_kept = own_kept + send(own_sent, "core", 1)
    own_sum = own_kept
    for step in range(1, NY):
        own_sum = own_sum + send(own_kept, "y", step)
    first = jnp.concatenate([first, own_sum], axis=1)
    first_x = [first, send(first, "x", -1), send(first, "x", 2), send(first, "x", 1)]
    first_x = place(first_x, "x", x).reshape(NX * wl, -1)
    indices = (row_index, col_index, near_index, far_index, crowd, my_slots, pos, keep)
    second_z, first_x, indices = lax.optimization_barrier((second_z, first_x, indices))
    row_index, col_index, near_index, far_index, crowd, my_slots, pos, keep = indices
    first_zx = ring_gather(first_x, "z")
    second_z = second_z.transpose(1, 0, 2, 3).reshape(2 * NZ * wl, rows)
    second_zx = ring_gather(second_z, "x")

    active = jnp.where(
        (row_index < 0)[:, None, None], ancestor.reshape(row_blocks, block, cols), 0
    ).reshape(rows, cols)
    q0 = place([mm(part[:, :rows], active) for part in first_zx], "z", z)
    q12 = place(
        [mm(part, active).reshape(2, NZ, wl, cols) for part in second_zx], "x", x, 2
    )
    q0 = q0.reshape(width, cols)
    q12 = q12.reshape(2 * width, cols)

    low = jnp.concatenate([q0, q12[:half]], axis=0)
    high = q12[half:]
    q_got = send(by_core(core, high, low), "core", 1)
    q_chip = by_core(core, low, high) + q_got

    def strip_of(owner):
        return lax.dynamic_slice_in_dim(q_chip, owner * block, block, axis=1)

    q_mine = strip_of(y)
    for step in range(1, NY):
        got = send(strip_of((y + step) % NY).astype(BF), "y", step)
        q_mine = q_mine + got.astype(F32)
    lane = (NX * x + (z // 2 - y - (y == 0)) % NY) * block
    p0, p12, own_mine = extract(first_zx, second_zx, z, x, lane, block, wl)
    p_rows = jnp.concatenate([p0[None], p12], axis=0)
    p_half = jnp.where(z % 2 == 0, p_rows[:, :half], p_rows[:, half:])
    pairs = []
    for fy in range(NY):
        for fc in range(NC):
            for fz in range(NZ):
                pair_z = (fy + fz // 2 + (fz < 2)) % NY
                target = ((fz // 2) * NC + fz % 2) * NZ + 2 * pair_z + fc
                pairs.append((target, (fy * NC + fc) * NZ + fz))
    p_half = lax.ppermute(p_half, ("y", "core", "z"), pairs)
    q_other = send(q_mine, "core", 1)
    q_low = by_core(core, q_mine, q_other)
    q_high = by_core(core, q_other, q_mine)
    q = (
        q_low[:width],
        jnp.concatenate([q_low[width:], q_high[:half]], axis=0),
        q_high[half:],
    )
    own_other = send(own_mine, "core", 1)
    own_all = jnp.concatenate(
        [by_core(core, own_mine, own_other), by_core(core, own_other, own_mine)], axis=1
    )
    own_all = lax.optimization_barrier(own_all)
    w10, w20, w21 = (own_all[:, i * width : (i + 1) * width] for i in range(3))

    u0 = jnp.where(keep[0], -q[0], 0.0).astype(BF)
    u1 = jnp.where(keep[1], -(q[1] + mm(w10, u0)), 0.0).astype(BF)
    u2 = jnp.where(keep[2], -(q[2] + mm(w20, u0) + mm(w21, u1)), 0.0).astype(BF)
    u = jnp.stack([u0, u1, u2])
    u_half = by_core(core, u[:, :half], u[:, half:])
    u_half, p_half = lax.optimization_barrier((u_half, p_half))

    p_other = send(p_half, "core", 1)
    p0, p1, p2 = (
        jnp.concatenate(
            [by_core(core, p_half[i], p_other[i]), by_core(core, p_other[i], p_half[i])],
            axis=0,
        )
        for i in range(S)
    )
    left = (by_core(core, p0, p2), by_core(core, p1, p2), by_core(core, p1, p2))
    right = (u0, by_core(core, u0, u1), by_core(core, u1, u2))
    part = jnp.concatenate([mmt(*pair) for pair in zip(left, right)], axis=0)
    strips = []
    for step in range(NY):
        strips.append(send(u_half, "y", NY - step) if step else u_half)
    pieces = part.reshape(NY * NX, 3 * width // (NY * NX), width)
    part = scatter_sum(pieces, ("y", "x"), y * NX + x)

    strip = jnp.stack(strips)
    strip_other = send(strip, "core", 1)
    ut = jnp.stack(
        [by_core(core, strip, strip_other), by_core(core, strip_other, strip)], axis=2
    ).reshape(NY, S * width, block)
    picked = pick(near_index, pos, ut).reshape(NX, 2, NODE, block, block)
    near = []
    for step in range(NX):
        pairs = []
        for fy in range(NY):
            for fc in range(NC):
                for fz in range(NZ):
                    for fx in range(NX):
                        target = ((fz // 2) * NC + fz % 2) * NZ + turn_z(fy, fc, fz, step)
                        pairs.append(
                            (((fy * NC + fc) * NZ + fz) * NX + fx, target * NX + (fx + step) % NX)
                        )
        near.append(lax.ppermute(picked[step], ("y", "core", "z", "x"), pairs))

    def more(ut):
        value = pick(far_index, pos, ut)
        pairs = []
        for fy in range(NY):
            for fc in range(NC):
                for fz in range(NZ):
                    target = ((fz // 2) * NC + fz % 2) * NZ + (fz + 2 * fy + fc) % NZ
                    pairs.append(((fy * NC + fc) * NZ + fz, target))
        value = lax.ppermute(value, ("y", "core", "z"), pairs)
        value = value.reshape(NX, 2 * NODE, block, block)
        value = lax.all_to_all(value, ("x",), 0, 0, tiled=True)
        return value.reshape(NX, 2, NODE, block, block)

    def none(ut):
        return jnp.zeros((NX, 2, NODE, block, block), BF)

    part, ut_late = lax.optimization_barrier((part, ut))
    far = lax.cond(crowd > 2, more, none, ut_late)
    part, far = lax.optimization_barrier((part, far))

    got = gather(part.astype(BF), ("z",), NZ)
    ids = jnp.arange(NZ, dtype=jnp.int32)[:, None, None]
    got = jnp.where(ids == z, part[None], got.astype(F32))
    part = jnp.sum(got, axis=0).astype(BF)
    cross = gather(part, ("y", "x"), NY * NX).reshape(3 * width, width)
    cross_other = send(cross, "core", 1)

    base = patch_strips(
        ancestor, ut, near, far, row_index, col_index, my_slots, pos
    )
    return patch_corner(base, cross, cross_other, diag_inverse, own_all, row_index, col_index, core)


def solution(mesh):
    fine = Mesh(mesh.devices.reshape(NY, NC, NZ, NX), ("y", "core", "z", "x"))
    row, col = ("y", "core"), ("z", "x")
    in_specs = (P(row, col), P(None, col, row), P(), P(), P())
    return jax.shard_map(
        update_all, mesh=fine, in_specs=in_specs, out_specs=P(row, col), check_vma=False
    )
```

```python
import jax
import jax.numpy as jnp
from jax import lax
from jax.experimental import pallas as pl
from jax.experimental.pallas import tpu as pltpu
from jax.sharding import Mesh, PartitionSpec as P

S = 3
NODE = 4
NY, NC, NZ, NX = 4, 2, 8, 4
SIZES = {"y": NY, "core": NC, "z": NZ, "x": NX}
BF = jnp.bfloat16
F32 = jnp.float32
PAIRS = ((0, 0), (1, 0), (1, 1), (2, 0), (2, 1), (2, 2))
INTERPRET = False


def send(value, axis, step):
    size = SIZES[axis]
    return lax.ppermute(value, axis, [(i, (i + step) % size) for i in range(size)])


def ring_gather(value, axis, begun=None):
    size = SIZES[axis]
    found = [None] * size
    found[0] = value
    ahead = behind = value
    for step in range(1, size // 2):
        if step == 1 and begun is not None:
            behind, ahead = begun
        else:
            behind = send(behind, axis, 1)
            ahead = send(ahead, axis, -1)
        found[step] = ahead
        found[size - step] = behind
    half = value.shape[0] // 2
    found[size // 2] = jnp.concatenate(
        [send(behind[:half], axis, 1), send(ahead[half:], axis, -1)], axis=0
    )
    return found


def place(found, axis, position, dim=0):
    size = SIZES[axis]
    out = None
    for step, part in enumerate(found):
        part = jnp.expand_dims(part, dim)
        if out is None:
            shape = list(part.shape)
            shape[dim] = size
            out = jnp.zeros(shape, part.dtype)
        out = lax.dynamic_update_slice_in_dim(out, part, (position + step) % size, axis=dim)
    return out


def scatter_sum(pieces, axes, position):
    count = pieces.shape[0]
    got = lax.all_to_all(pieces.astype(BF), axes, 0, 0, tiled=True).astype(F32)
    ids = jnp.arange(count, dtype=jnp.int32)[:, None, None]
    return jnp.sum(jnp.where(ids == position, pieces, got), axis=0)


def gather(value, axes, count):
    spread = jnp.broadcast_to(value[None], (count, *value.shape))
    return lax.all_to_all(spread, axes, 0, 0, tiled=True)


def by_core(core, first, second):
    return jnp.where(core == 0, first, second)


def prepare_kernel(flags, at, p_ref, first_ref, second_ref, own_ref):
    block = own_ref.shape[1] // (3 * NODE)
    row_blocks = p_ref.shape[2] // block
    for s in range(S):
        for b in range(row_blocks):
            span = slice(b * block, (b + 1) * block)
            value = p_ref[s, :, span]
            value = jnp.where(flags[s * row_blocks + b] > 0, value, jnp.zeros_like(value))
            if s == 0:
                first_ref[:, span] = value
            else:
                second_ref[0, s - 1, :, span] = value

    def spread(n, carry):
        second_ref[n] = second_ref[0]
        return carry

    lax.fori_loop(1, NZ, spread, 0)
    for pair, (s, t) in enumerate(((1, 0), (2, 0), (2, 1))):
        for k in range(NODE):
            index = at[t * NODE + k]
            inside = (index >= 0) & (index < row_blocks)
            start = pl.multiple_of(jnp.where(inside, index, 0) * block, block)
            value = p_ref[s, :, pl.ds(start, block)]
            value = jnp.where(inside, value, jnp.zeros_like(value))
            own_ref[:, (pair * NODE + k) * block : (pair * NODE + k + 1) * block] = value


def prepare(panels, listed, at, block):
    _, wl, rows = panels.shape
    return pl.pallas_call(
        prepare_kernel,
        out_shape=(
            jax.ShapeDtypeStruct((wl, rows), BF),
            jax.ShapeDtypeStruct((NZ, 2, wl, rows), BF),
            jax.ShapeDtypeStruct((wl, 3 * NODE * block), BF),
        ),
        in_specs=[
            pl.BlockSpec(memory_space=pltpu.SMEM),
            pl.BlockSpec(memory_space=pltpu.SMEM),
            pl.BlockSpec(memory_space=pltpu.VMEM),
        ],
        interpret=INTERPRET,
    )(listed.astype(jnp.int32).reshape(-1), at, panels)


def extract_kernel(pos, *refs):
    first, second = refs[:NZ], refs[NZ : NZ + NX]
    p0, p12, own = refs[NZ + NX :]
    rows = second[0].shape[3]
    block = p0.shape[2]
    lane = pl.multiple_of(pos[2], block)
    for d, ref in enumerate(first):
        at = (pos[0] + d) % NZ
        own[at] = ref[:, rows:]

        @pl.when(at // (NZ // 2) == pos[3])
        def _(ref=ref, at=at):
            p0[at % (NZ // 2)] = ref[:, pl.ds(lane, block)]

    for d, ref in enumerate(second):
        at = (pos[1] + d) % NX
        part = ref[:, pl.ds(pos[3] * (NZ // 2), NZ // 2), :, pl.ds(lane, block)]
        p12[:, :, pl.ds(at, 1)] = part[:, :, None]


def extract(first_zx, second_zx, z, x, lane, block, wl):
    second_zx = [part.reshape(2, NZ, wl, -1) for part in second_zx]
    extra = first_zx[0].shape[1] - second_zx[0].shape[3]
    vmem = pl.BlockSpec(memory_space=pltpu.VMEM)
    p0, p12, own = pl.pallas_call(
        extract_kernel,
        out_shape=(
            jax.ShapeDtypeStruct((NZ // 2, NX * wl, block), BF),
            jax.ShapeDtypeStruct((2, NZ // 2, NX, wl, block), BF),
            jax.ShapeDtypeStruct((NZ, NX * wl, extra), BF),
        ),
        in_specs=[pl.BlockSpec(memory_space=pltpu.SMEM), *[vmem] * (NZ + NX)],
        out_specs=(vmem, vmem, vmem),
        interpret=INTERPRET,
    )(jnp.stack([z, x, lane, z % 2]).astype(jnp.int32), *first_zx, *second_zx)
    half = NZ * NX * wl // 2
    panel = jnp.concatenate([p0.reshape(1, half, block), p12.reshape(2, half, block)], axis=0)
    return panel, own.reshape(2 * half, extra)


def pick_kernel(index, pos, ut_ref, out_ref):
    block = ut_ref.shape[2]

    def step(i, carry):
        start = pl.multiple_of(index[i] * block, block)
        for q in range(NODE):
            out_ref[i, q] = ut_ref[(q - pos[1] + NY) % NY, pl.ds(start, block), :]
        return carry

    lax.fori_loop(0, out_ref.shape[0], step, 0)


def pick(index, pos, ut):
    block = ut.shape[2]
    return pl.pallas_call(
        pick_kernel,
        out_shape=jax.ShapeDtypeStruct((index.shape[0], NODE, block, block), BF),
        in_specs=[
            pl.BlockSpec(memory_space=pltpu.SMEM),
            pl.BlockSpec(memory_space=pltpu.SMEM),
            pl.BlockSpec(memory_space=pltpu.VMEM),
        ],
        interpret=INTERPRET,
    )(index, pos, ut)


def strips_kernel(rs, cs, slots, pos, ut, *refs):
    near = refs[:NX]
    far, _, out, buffer, sem_col, sem_row = refs[NX:]
    block = ut.shape[2]
    row_blocks = rs.shape[0]

    def column(j):
        return pltpu.make_async_copy(
            buffer.at[j], out.at[:, pl.ds(j * block, block)], sem_col.at[j]
        )

    for j in range(NODE):
        slot = slots[j]

        @pl.when(cs[j] >= 0)
        def _(j=j, slot=slot):
            for step in range(NX):
                i = (pos[0] - step + NX) % NX

                def fill(q, carry, j=j, slot=slot, step=step, i=i):
                    at = pl.multiple_of((i * NODE + q) * block, block)
                    tile = jnp.where(
                        slot < 2,
                        near[step][jnp.minimum(slot, 1), q],
                        far[i, jnp.maximum(slot - 2, 0), q],
                    )
                    buffer[j, pl.ds(at, block), :] = tile.astype(F32).T.astype(BF)
                    return carry

                lax.fori_loop(0, NODE, fill, 0)
            column(j).start()

    for j in range(NODE):

        @pl.when(cs[j] >= 0)
        def _(j=j):
            column(j).wait()

    def each(act):
        def step(i, carry):
            row = rs[i]

            @pl.when(row >= 0)
            def _():
                for j in range(NODE):
                    act(
                        pltpu.make_async_copy(
                            ut.at[(j - pos[1] + NY) % NY, pl.ds(row * block, block), :],
                            out.at[pl.ds(i * block, block), pl.ds(j * block, block)],
                            sem_row,
                        )
                    )

            return carry

        lax.fori_loop(0, row_blocks, step, 0)

    each(lambda copy: copy.start())
    each(lambda copy: copy.wait())


def patch_strips(ancestor, ut, near, far, row_index, col_index, slots, pos):
    rows, cols = ancestor.shape
    block = cols // NODE
    smem = pl.BlockSpec(memory_space=pltpu.SMEM)
    vmem = pl.BlockSpec(memory_space=pltpu.VMEM)
    anywhere = pl.BlockSpec(memory_space=pl.ANY)
    return pl.pallas_call(
        strips_kernel,
        out_shape=jax.ShapeDtypeStruct((rows, cols), BF),
        in_specs=[smem, smem, smem, smem, *[vmem] * (NX + 2), anywhere],
        out_specs=anywhere,
        scratch_shapes=[
            pltpu.VMEM((NODE, rows, block), BF),
            pltpu.SemaphoreType.DMA((NODE,)),
            pltpu.SemaphoreType.DMA,
        ],
        input_output_aliases={NX + 6: 0},
        interpret=INTERPRET,
    )(row_index, col_index, slots, pos, ut, *near, far, ancestor)


def corner_kernel(
    rs, cs, core, mine, other, diag, own, base, out, cross, kk, sem
):
    width = diag.shape[1]
    block = width // NODE
    for i in range(6):
        rows = slice((i % 3) * width, (i % 3 + 1) * width)
        cross[i] = jnp.where(core[0] == i // 3, mine[rows], other[rows]).astype(F32)
    c = {pair: cross.at[i] for i, pair in enumerate(PAIRS)}
    w10, w20, w21 = (own.at[:, i * width : (i + 1) * width] for i in range(3))

    def at(s, t):
        return kk.at[s * width : (s + 1) * width, t * width : (t + 1) * width]

    def diagonal(s, value):
        return (diag[s] - 0.5 * (value + value.T)).astype(BF)

    def keep(s, t, value):
        at(s, t)[...] = value.astype(BF)
        at(t, s)[...] = value.T.astype(BF)

    at(0, 0)[...] = diagonal(0, c[0, 0][...])
    keep(1, 0, -(c[1, 0][...] + mm(w10[...], at(0, 0)[...])))
    at(1, 1)[...] = diagonal(1, c[1, 1][...] + mm(w10[...], at(0, 1)[...]))
    keep(2, 0, -(c[2, 0][...] + mm(w20[...], at(0, 0)[...]) + mm(w21[...], at(1, 0)[...])))
    keep(2, 1, -(c[2, 1][...] + mm(w20[...], at(0, 1)[...]) + mm(w21[...], at(1, 1)[...])))
    at(2, 2)[...] = diagonal(
        2, c[2, 2][...] + mm(w20[...], at(0, 2)[...]) + mm(w21[...], at(1, 2)[...])
    )

    def each(act):
        def step(i, carry):
            row = rs[i]
            for j in range(NODE):
                col = cs[j]

                @pl.when((row >= 0) & (col >= 0))
                def _():
                    copy = pltpu.make_async_copy(
                        kk.at[pl.ds(row * block, block), pl.ds(col * block, block)],
                        out.at[pl.ds(i * block, block), pl.ds(j * block, block)],
                        sem,
                    )
                    act(copy)

            return carry

        lax.fori_loop(0, rs.shape[0], step, 0)

    each(lambda copy: copy.start())
    each(lambda copy: copy.wait())


def patch_corner(base, mine, other, diag_inverse, own, row_index, col_index, core):
    width = diag_inverse.shape[1]
    smem = pl.BlockSpec(memory_space=pltpu.SMEM)
    vmem = pl.BlockSpec(memory_space=pltpu.VMEM)
    anywhere = pl.BlockSpec(memory_space=pl.ANY)
    return pl.pallas_call(
        corner_kernel,
        out_shape=jax.ShapeDtypeStruct(base.shape, BF),
        in_specs=[smem, smem, smem, vmem, vmem, vmem, vmem, anywhere],
        out_specs=anywhere,
        scratch_shapes=[
            pltpu.VMEM((6, width, width), F32),
            pltpu.VMEM((S * width, S * width), BF),
            pltpu.SemaphoreType.DMA,
        ],
        input_output_aliases={7: 0},
        interpret=INTERPRET,
    )(row_index, col_index, core.astype(jnp.int32).reshape(1), mine, other, diag_inverse, own, base)


def contract(left, right, dims):
    return lax.dot_general(left, right, (dims, ((), ())), preferred_element_type=F32)


def mm(left, right):
    return contract(left, right, ((1,), (0,)))


def mmt(left, right):
    return contract(left, right, ((1,), (1,)))


def update_all(ancestor, panels, diag_inverse, supernode_blocks, row_lists):
    y, core, z, x = (lax.axis_index(name) for name in ("y", "core", "z", "x"))
    rows, cols = ancestor.shape
    block = cols // NODE
    width = NODE * block
    half = width // 2
    wl = panels.shape[1]
    row_blocks = rows // block
    group = 2 * y + core
    first_row = group * row_blocks
    first_col = (NX * z + x) * NODE
    k_list = supernode_blocks.reshape(-1)
    numbers = jnp.arange(S * NODE, dtype=jnp.int32) + 1

    def number_in(ids):
        return jnp.sum(jnp.where(ids[:, None] == k_list[None, :], numbers, 0), axis=1) - 1

    row_ids = first_row + jnp.arange(row_blocks, dtype=jnp.int32)
    row_index = number_in(row_ids)
    col_index = number_in(first_col + jnp.arange(NODE, dtype=jnp.int32))
    listed = jnp.any(row_ids[None, :, None] == row_lists[:, None, :], axis=2)

    def turn_z(fy, fc, fz, step):
        return (fz + 2 * fy + fc + 2 * step + (1 if fz == 0 else 0)) % NZ

    def slots_of(z_at, x_at):
        found = number_in((NX * z_at + x_at) * NODE + jnp.arange(NODE, dtype=jnp.int32))
        rank = jnp.cumsum((found >= 0).astype(jnp.int32)) - 1
        ids = jnp.arange(NODE, dtype=jnp.int32)[:, None]
        hit = (found >= 0)[None, :] & (rank[None, :] == ids)
        return jnp.sum(jnp.where(hit, found[None, :], 0), axis=1), rank

    shift = z + group + jnp.where(z == 0, 1, 0)
    near_index = jnp.concatenate(
        [slots_of((shift + 2 * step) % NZ, (x + step) % NX)[0][:2] for step in range(NX)]
    )
    far_index = jnp.concatenate([slots_of((z + group) % NZ, at)[0][2:] for at in range(NX)])
    owners = k_list // NODE
    crowd = jnp.max(jnp.sum((owners[:, None] == owners[None, :]).astype(jnp.int32), axis=1))
    my_slots = slots_of(z, x)[1]
    pos = jnp.stack([x, y]).astype(jnp.int32)
    my_block = first_col + y
    outside = jnp.all(my_block != k_list)
    keep = jnp.any(my_block == row_lists, axis=1) & outside

    first, second, own = prepare(panels, listed, k_list - first_row, block)

    lane_half = 3 * half
    own_kept = by_core(core, own[:, :lane_half], own[:, lane_half:])
    own_sent = by_core(core, own[:, lane_half:], own[:, :lane_half])
    second_z = lax.all_to_all(second, ("z",), 0, 0, tiled=True)
    own_kept = own_kept + send(own_sent, "core", 1)
    own_sum = own_kept
    for step in range(1, NY):
        own_sum = own_sum + send(own_kept, "y", step)
    first = jnp.concatenate([first, own_sum], axis=1)
    first_x = [first, send(first, "x", -1), send(first, "x", 2), send(first, "x", 1)]
    first_x = place(first_x, "x", x).reshape(NX * wl, -1)
    indices = (row_index, col_index, near_index, far_index, crowd, my_slots, pos, keep)
    second_z, first_x, indices, late = lax.optimization_barrier(
        (second_z, first_x, indices, ancestor)
    )
    row_index, col_index, near_index, far_index, crowd, my_slots, pos, keep = indices
    first_zx = ring_gather(first_x, "z")
    second_z = second_z.transpose(1, 0, 2, 3).reshape(2 * NZ * wl, rows)
    second_zx = ring_gather(second_z, "x")

    active = jnp.where(
        (row_index < 0)[:, None, None], ancestor.reshape(row_blocks, block, cols), 0
    ).reshape(rows, cols)
    q0 = place([mm(part[:, :rows], active) for part in first_zx], "z", z)
    q12 = place(
        [mm(part, active).reshape(2, NZ, wl, cols) for part in second_zx], "x", x, 2
    )
    q0 = q0.reshape(width, cols)
    q12 = q12.reshape(2 * width, cols)

    low = jnp.concatenate([q0, q12[:half]], axis=0)
    high = q12[half:]
    q_got = send(by_core(core, high, low), "core", 1)
    q_chip = by_core(core, low, high) + q_got

    def strip_of(owner):
        return lax.dynamic_slice_in_dim(q_chip, owner * block, block, axis=1)

    q_mine = strip_of(y)
    for step in range(1, NY):
        got = send(strip_of((y + step) % NY).astype(BF), "y", step)
        q_mine = q_mine + got.astype(F32)
    lane = (NX * x + (z // 2 - y - (y == 0)) % NY) * block
    p_half, own_mine = extract(first_zx, second_zx, z, x, lane, block, wl)
    pairs = []
    for fy in range(NY):
        for fc in range(NC):
            for fz in range(NZ):
                pair_z = (fy + fz // 2 + (fz < 2)) % NY
                target = ((fz // 2) * NC + fz % 2) * NZ + 2 * pair_z + fc
                pairs.append((target, (fy * NC + fc) * NZ + fz))
    p_half = lax.ppermute(p_half, ("y", "core", "z"), pairs)
    q_other = send(q_mine, "core", 1)
    q_low = by_core(core, q_mine, q_other)
    q_high = by_core(core, q_other, q_mine)
    q = (
        q_low[:width],
        jnp.concatenate([q_low[width:], q_high[:half]], axis=0),
        q_high[half:],
    )
    own_other = send(own_mine, "core", 1)
    own_all = jnp.concatenate(
        [by_core(core, own_mine, own_other), by_core(core, own_other, own_mine)], axis=1
    )
    own_all = lax.optimization_barrier(own_all)
    w10, w20, w21 = (own_all[:, i * width : (i + 1) * width] for i in range(3))

    u0 = jnp.where(keep[0], -q[0], 0.0).astype(BF)
    u1 = jnp.where(keep[1], -(q[1] + mm(w10, u0)), 0.0).astype(BF)
    u2 = jnp.where(keep[2], -(q[2] + mm(w20, u0) + mm(w21, u1)), 0.0).astype(BF)
    u = jnp.stack([u0, u1, u2])
    u_half = by_core(core, u[:, :half], u[:, half:])
    u_half, p_half = lax.optimization_barrier((u_half, p_half))

    p_other = send(p_half, "core", 1)
    p0, p1, p2 = (
        jnp.concatenate(
            [by_core(core, p_half[i], p_other[i]), by_core(core, p_other[i], p_half[i])],
            axis=0,
        )
        for i in range(S)
    )
    left = (by_core(core, p0, p2), by_core(core, p1, p2), by_core(core, p1, p2))
    right = (u0, by_core(core, u0, u1), by_core(core, u1, u2))
    part = jnp.concatenate([mmt(*pair) for pair in zip(left, right)], axis=0)
    strips = []
    for step in range(NY):
        strips.append(send(u_half, "y", NY - step) if step else u_half)
    pieces = part.reshape(NY * NX, 3 * width // (NY * NX), width)
    part = scatter_sum(pieces, ("y", "x"), y * NX + x)

    strip = jnp.stack(strips)
    strip_other = send(strip, "core", 1)
    ut = jnp.stack(
        [by_core(core, strip, strip_other), by_core(core, strip_other, strip)], axis=2
    ).reshape(NY, S * width, block)
    picked = pick(near_index, pos, ut).reshape(NX, 2, NODE, block, block)
    near = []
    for step in range(NX):
        pairs = []
        for fy in range(NY):
            for fc in range(NC):
                for fz in range(NZ):
                    for fx in range(NX):
                        target = ((fz // 2) * NC + fz % 2) * NZ + turn_z(fy, fc, fz, step)
                        pairs.append(
                            (((fy * NC + fc) * NZ + fz) * NX + fx, target * NX + (fx + step) % NX)
                        )
        near.append(lax.ppermute(picked[step], ("y", "core", "z", "x"), pairs))

    def more(ut):
        value = pick(far_index, pos, ut)
        pairs = []
        for fy in range(NY):
            for fc in range(NC):
                for fz in range(NZ):
                    target = ((fz // 2) * NC + fz % 2) * NZ + (fz + 2 * fy + fc) % NZ
                    pairs.append(((fy * NC + fc) * NZ + fz, target))
        value = lax.ppermute(value, ("y", "core", "z"), pairs)
        value = value.reshape(NX, 2 * NODE, block, block)
        value = lax.all_to_all(value, ("x",), 0, 0, tiled=True)
        return value.reshape(NX, 2, NODE, block, block)

    def none(ut):
        return jnp.zeros((NX, 2, NODE, block, block), BF)

    part, ut_late = lax.optimization_barrier((part, ut))
    far = lax.cond(crowd > 2, more, none, ut_late)
    part, far = lax.optimization_barrier((part, far))

    got = gather(part.astype(BF), ("z",), NZ)
    ids = jnp.arange(NZ, dtype=jnp.int32)[:, None, None]
    got = jnp.where(ids == z, part[None], got.astype(F32))
    part = jnp.sum(got, axis=0).astype(BF)
    cross = gather(part, ("y", "x"), NY * NX).reshape(3 * width, width)
    cross_other = send(cross, "core", 1)

    base = patch_strips(
        late, ut, near, far, row_index, col_index, my_slots, pos
    )
    return patch_corner(base, cross, cross_other, diag_inverse, own_all, row_index, col_index, core)


def solution(mesh):
    fine = Mesh(mesh.devices.reshape(NY, NC, NZ, NX), ("y", "core", "z", "x"))
    row, col = ("y", "core"), ("z", "x")
    in_specs = (P(row, col), P(None, col, row), P(), P(), P())
    return jax.shard_map(
        update_all, mesh=fine, in_specs=in_specs, out_specs=P(row, col), check_vma=False
    )
```
